256 devices in a mesh: gx: 32 (over x, z), gy: 8 (over y, core).
Axes of the slice: x: 4, y: 4, z: 8, core: 2. Of those that a mesh axis runs over, the one named last changes fastest.
Arguments:
- flow_state: float32 [4, 4096, 1024], P(None, 'gx', 'gy'), may hold values from -6 to 6
- sound_speed_sq: float32 [4096, 1024], P('gx', 'gy'), may hold values from 0.25 to 1
- snapshots: bfloat16 [62, 4096, 1024], P(None, 'gx', 'gy'), may hold values from -96 to 96
Outputs:
- new_state: float32 [4, 4096, 1024], P(None, 'gx', 'gy')
- pod_basis: float32 [64, 4096, 1024], P(None, 'gx', 'gy')
The draws below stay inside these ranges and needn't reach their ends.
All inputs are finite; a program needn't handle non-finite values.
Results may differ from the reference program's by a relative error of at most 0.00063.
Values sent between devices are 32-bit elements; how exact they have to be, the bound alone decides.
A program may use at most 64 MiB of HBM per device.

```python
import math
import jax
import jax.numpy as jnp
from jax import lax

MODES = 64
STEPS = 2
RESIDENT = 62
NX = 4096
NY = 1024


def draw_snapshots(key, part):
    subkeys = jax.random.split(key, 5)
    array_shape = (RESIDENT, NX, NY)
    row_x = jnp.arange(NX, dtype=jnp.float32)[None, :, None] / NX
    row_y = jnp.arange(NY, dtype=jnp.float32)[None, None, :] / NY
    envelope = jnp.exp(math.log(10.0) * row_x)
    wave_x = jax.random.randint(subkeys[0], (RESIDENT, 1, 1), 1, 9).astype(jnp.float32)
    wave_y = jax.random.randint(subkeys[1], (RESIDENT, 1, 1), 1, 5).astype(jnp.float32)
    phase_shift = jax.random.uniform(subkeys[2], (RESIDENT, 1, 1), minval=-math.pi, maxval=math.pi)
    column_scale = jnp.exp(jax.random.uniform(subkeys[3], (RESIDENT, 1, 1), minval=math.log(0.3), maxval=math.log(3.0)))
    coherent = 0.8 * jnp.cos(2.0 * math.pi * (wave_x * row_x + wave_y * row_y) + phase_shift)
    rough_part = 0.6 * jax.random.truncated_normal(subkeys[4], -4.0, 4.0, array_shape)
    return (envelope * column_scale * (rough_part + coherent)).astype(jnp.bfloat16)


def level_of(stream_key, shape, cuts, smallest, largest):
    level, own = 1.0, jax.random.fold_in(stream_key, 6)
    for dim, parts in cuts:
        steps = jnp.exp(jax.random.uniform(jax.random.fold_in(own, dim), (parts,), jnp.float32, smallest / len(cuts), largest / len(cuts)))
        level = level * jnp.repeat(steps, shape[dim] // parts).reshape([-1 if axis == dim else 1 for axis in range(len(shape))])
    return level


def normal_values(key, dims, scale, most, shards=(), held_as=jnp.bfloat16):
    result = jax.random.normal(key, dims, jnp.float32) * scale
    if len(shards) > 0:
        result = level_of(key, dims, shards, -0.22, 0.18) * result
    return jnp.clip(result, min=-most, max=most).astype(held_as)


def setup_inputs(seed: int = 0) -> dict:
    streams_of = jax.random.split(jax.random.key(seed), 4)
    return {
        "flow_state": normal_values(streams_of[0], (4, NX, NY), 1.0, 6.0, ((1, 32), (2, 8)), jnp.float32),
        "sound_speed_sq": jnp.clip(jnp.exp(math.log(1.0) - 1.3862944 * jax.random.uniform(streams_of[1], (NX, NY), jnp.float32) ** level_of(streams_of[1], (NX, NY), ((0, 32), (1, 8)), -0.2, 0.2)), 0.25, 1.0),
        "snapshots": draw_snapshots(jax.random.fold_in(streams_of[3], 71), 0),
    }


courant = 0.8
stream_speed = 0.3
span_speed = 0.1

def derivative_x(padded):
    interior = padded[:, :, 2:-2]
    extent = interior.shape[1] - 4
    ahead_one = interior[:, 3:3 + extent]
    behind_one = interior[:, 1:1 + extent]
    ahead_two = interior[:, 4:4 + extent]
    behind_two = interior[:, 0:extent]
    return (8.0 * (ahead_one - behind_one) - (ahead_two - behind_two)) / 12.0

def derivative_y(padded):
    interior = padded[:, 2:-2, :]
    extent = interior.shape[2] - 4
    ahead_one = interior[:, :, 3:3 + extent]
    behind_one = interior[:, :, 1:1 + extent]
    ahead_two = interior[:, :, 4:4 + extent]
    behind_two = interior[:, :, 0:extent]
    return (8.0 * (ahead_one - behind_one) - (ahead_two - behind_two)) / 12.0

def tendency(padded, sound_sq):
    slope_x = derivative_x(padded)
    slope_y = derivative_y(padded)
    advect = stream_speed * slope_x + span_speed * slope_y
    diverge = slope_x[1] + slope_y[2]
    rate_rho = -courant * (advect[0] + diverge)
    rate_mx = -courant * (advect[1] + slope_x[3])
    rate_my = -courant * (advect[2] + slope_y[3])
    rate_p = -courant * (advect[3] + sound_sq * diverge)
    return jnp.stack([rate_rho, rate_mx, rate_my, rate_p])

def extend(current):
    return jnp.pad(current, ((0, 0), (2, 2), (2, 2)), mode='wrap')

def advance(current, sound_sq):
    first = current + tendency(extend(current), sound_sq)
    second = 0.75 * current + 0.25 * (first + tendency(extend(first), sound_sq))
    return 1.0 / 3.0 * current + 2.0 / 3.0 * (second + tendency(extend(second), sound_sq))

def reference(flow_state, sound_speed_sq, snapshots):
    current = flow_state
    columns = [snapshots]
    for step_index in range(STEPS):
        current = advance(current, sound_speed_sq)
        columns.append(current[3].astype(jnp.bfloat16)[None])
    snap_block = jnp.concatenate(columns, axis=0)
    flat_block = snap_block.reshape(MODES, -1).astype(jnp.float32)
    gram = jnp.dot(flat_block, flat_block.T, precision=lax.Precision.HIGHEST) / (NX * NY)
    lower_factor = jnp.linalg.cholesky(gram)
    identity_matrix = jnp.eye(MODES, dtype=jnp.float32)
    inverse = jax.scipy.linalg.solve_triangular(lower_factor, identity_matrix, lower=True)
    pod_basis = jnp.dot(inverse, flat_block, precision=lax.Precision.HIGHEST).reshape(MODES, NX, NY)
    return (current, pod_basis)
```

```python
import functools

import jax
import jax.numpy as jnp
from jax import lax
from jax.experimental import pallas as pl
from jax.experimental.pallas import tpu as pltpu
from jax.sharding import PartitionSpec as P

MESH = pl.DeviceIdType.MESH
STEPS = 2
courant = 0.8
stream_speed = 0.3
span_speed = 0.1

MODES = 64
RESIDENT = 62
TILE = 128
HALO = 12
PAD = 16
ROWS = TILE + 2 * PAD
FIELDS = 5
GX = 32
GY = 8


def lanes(shape):
    return lax.broadcasted_iota(jnp.int32, shape, len(shape) - 1)


def slope_x(ref, field, row, rows):
    near = ref[field, pl.ds(row + 1, rows), :] - ref[field, pl.ds(row - 1, rows), :]
    far = ref[field, pl.ds(row + 2, rows), :] - ref[field, pl.ds(row - 2, rows), :]
    return (2.0 / 3.0) * near - (1.0 / 12.0) * far


def slope_y(main, edge, first, last):
    def pair(amount):
        a, b = pltpu.roll(main, amount, 1), pltpu.roll(edge, amount, 1)
        wrapped = last[amount] if amount > 64 else first[amount]
        return jnp.where(wrapped, b, a), jnp.where(wrapped, a, b)

    ahead_one, behind_one = pair(TILE - 1), pair(1)
    ahead_two, behind_two = pair(TILE - 2), pair(2)
    return tuple(
        (2.0 / 3.0) * (a1 - b1) - (1.0 / 12.0) * (a2 - b2)
        for a1, b1, a2, b2 in zip(ahead_one, behind_one, ahead_two, behind_two)
    )


def stage(kind, state, source, target, sound):
    rows = 8
    lane = lanes((rows, TILE))
    first = {1: lane < 1, 2: lane < 2}
    last = {TILE - 1: lane >= TILE - 1, TILE - 2: lane >= TILE - 2}

    def chunk(index, carry):
        row = pl.multiple_of(8 + index * rows, rows)
        here = pl.ds(row, rows)
        centre = [[source[s][f, here, :] for f in range(4)] for s in range(2)]
        dx = [[slope_x(source[s], f, row, rows) for f in range(4)] for s in range(2)]
        both = [slope_y(centre[0][f], centre[1][f], first, last) for f in range(4)]
        for s in range(2):
            dy = [both[f][s] for f in range(4)]
            diverge = dx[s][1] + dy[2]
            advect = [stream_speed * dx[s][f] + span_speed * dy[f] for f in range(4)]
            rate = [
                advect[0] + diverge,
                advect[1] + dx[s][3],
                advect[2] + dy[3],
                advect[3] + sound[s][4, here, :] * diverge,
            ]
            for f in range(4):
                moved = centre[s][f] - courant * rate[f]
                if kind == 2:
                    moved = 0.75 * state[s][f, here, :] + 0.25 * moved
                elif kind == 3:
                    moved = (1.0 / 3.0) * state[s][f, here, :] + (2.0 / 3.0) * moved
                target[s][f, here, :] = moved
        return carry

    lax.fori_loop(0, (ROWS - 16) // rows, chunk, 0)


def wide_kernel(
    flow_hbm, sound_hbm, snap_hbm, state_out, block_out, gram_out,
    snap, block, tile, edge, first_main, first_edge, second_main, second_edge,
    strip, left_strip, right_strip, packed, part_one, part_two, total_two, whole,
    load_sem, halo_send, halo_recv, sum_send, sum_recv,
):
    gx, gy = lax.axis_index("gx"), lax.axis_index("gy")
    core = lax.rem(gy, 2)

    def at(dx, dy):
        return (lax.rem(gx + (dx + GX), GX), lax.rem(gy + (dy + GY), GY))

    row_peers = [at(d, 0) for d in range(1, GX)]
    column_peers = [at(0, d) for d in range(1, GY)]
    corner_peers = [at(dx, dy) for dx in (-1, 1) for dy in (-1, 1)]
    everyone = row_peers + column_peers + corner_peers

    barrier = pltpu.get_barrier_semaphore()
    for peer in everyone:
        pl.semaphore_signal(barrier, inc=1, device_id=peer, device_id_type=MESH)

    inside = pl.ds(PAD, TILE)
    loads = [
        pltpu.make_async_copy(flow_hbm, tile.at[pl.ds(0, 4), inside, :], load_sem.at[0]),
        pltpu.make_async_copy(sound_hbm, tile.at[4, inside, :], load_sem.at[1]),
        pltpu.make_async_copy(snap_hbm, snap.at[pl.ds(0, RESIDENT)], load_sem.at[2]),
    ]
    for load in loads:
        load.start()
    loads[0].wait()
    loads[1].wait()

    def pack(index, carry):
        row = pl.multiple_of(index * 16, 16)
        lane = lanes((16, TILE))
        gathered = pltpu.roll(tile[0, pl.ds(PAD + row, 16), :], HALO, 1)
        for f in range(1, FIELDS):
            moved = pltpu.roll(tile[f, pl.ds(PAD + row, 16), :], HALO + 24 * f, 1)
            gathered = jnp.where(lane >= 24 * f, moved, gathered)
        strip[pl.ds(row, 16), :] = gathered
        return carry

    lax.fori_loop(0, TILE // 16, pack, 0)
    pl.semaphore_wait(barrier, len(everyone))

    top, bottom = pl.ds(0, PAD), pl.ds(PAD + TILE, PAD)
    low, high = pl.ds(0, PAD), pl.ds(TILE - PAD, PAD)
    moves = [
        (tile.at[:, pl.ds(TILE, PAD), :], tile.at[:, top, :], at(1, 0)),
        (tile.at[:, pl.ds(PAD, PAD), :], tile.at[:, bottom, :], at(-1, 0)),
        (strip, left_strip.at[inside, :], at(0, 1)),
        (strip, right_strip.at[inside, :], at(0, -1)),
        (strip.at[high, :], left_strip.at[top, :], at(1, 1)),
        (strip.at[low, :], left_strip.at[bottom, :], at(-1, 1)),
        (strip.at[high, :], right_strip.at[top, :], at(1, -1)),
        (strip.at[low, :], right_strip.at[bottom, :], at(-1, -1)),
    ]
    halos = []
    for number, (source, target, peer) in enumerate(moves):
        halos.append(
            pltpu.make_async_remote_copy(
                src_ref=source, dst_ref=target, send_sem=halo_send.at[number],
                recv_sem=halo_recv.at[number], device_id=peer, device_id_type=MESH,
            )
        )
        halos[-1].start()

    loads[2].wait()

    for group in range(3):
        modes = pl.ds(group * 16, 16)
        for row in range(0, TILE, 16):
            turned = jnp.swapaxes(snap[modes, row : row + 16, :], 0, 1)
            for i in range(16):
                block[modes, (row + i) * TILE : (row + i + 1) * TILE] = turned[i]

    for halo in halos:
        halo.wait()

    def unpack(index, carry):
        here = pl.ds(pl.multiple_of(index * 16, 16), 16)
        lane = lanes((16, TILE))
        merged = jnp.where(lax.rem(lane, 24) >= HALO, right_strip[here, :], left_strip[here, :])
        for f in range(FIELDS):
            edge[f, here, :] = pltpu.roll(merged, TILE - (24 * f + HALO), 1)
        return carry

    lax.fori_loop(0, ROWS // 16, unpack, 0)

    state = (tile, edge)
    one, two = (first_main, first_edge), (second_main, second_edge)
    pressures = []
    for step in range(STEPS):
        stage(1, state, state, one, state)
        stage(2, state, one, two, state)
        stage(3, state, two, state, state)
        snap[RESIDENT + step] = tile[3, inside, :].astype(jnp.bfloat16)

    state_out[...] = tile[0:4, inside, :]

    last = pl.ds(48, 16)
    for row in range(0, TILE, 16):
        turned = jnp.swapaxes(snap[last, row : row + 16, :], 0, 1)
        for i in range(16):
            block[last, (row + i) * TILE : (row + i + 1) * TILE] = turned[i]

    save = pltpu.make_async_copy(block, block_out, load_sem.at[2])
    save.start()
    gram = lax.dot_general(
        block[...], block[...], (((1,), (1,)), ((), ())), preferred_element_type=jnp.float32
    ) * (1.0 / (GX * GY * TILE * TILE))
    folded = jnp.concatenate([gram[32:64], gram[0:32]], axis=1)
    packed[0] = folded[0:16]
    packed[1] = folded[16:32]

    for number, peer in enumerate(column_peers):
        pltpu.make_async_remote_copy(
            src_ref=packed.at[lax.rem(peer[1], 2)], dst_ref=part_one.at[number],
            send_sem=sum_send.at[0], recv_sem=sum_recv.at[0], device_id=peer, device_id_type=MESH,
        ).start()
    pltpu.make_async_copy(part_one, part_one, sum_recv.at[0]).wait()
    total = packed[core]
    for number in range(GY - 1):
        total = total + part_one[number]
    total_two[...] = total
    pltpu.make_async_copy(part_one, part_one, sum_send.at[0]).wait()

    for number, peer in enumerate(row_peers):
        pltpu.make_async_remote_copy(
            src_ref=total_two, dst_ref=part_two.at[number],
            send_sem=sum_send.at[1], recv_sem=sum_recv.at[1], device_id=peer, device_id_type=MESH,
        ).start()
    pltpu.make_async_copy(part_two, part_two, sum_recv.at[1]).wait()

    def add(number, so_far):
        return so_far + part_two[number]

    total = lax.fori_loop(0, GX - 1, add, total_two[...])
    pltpu.make_async_copy(part_two, part_two, sum_send.at[1]).wait()
    whole[core] = total

    partner = (gx, gy + 1 - 2 * core)
    swap = pltpu.make_async_remote_copy(
        src_ref=whole.at[core], dst_ref=whole.at[core],
        send_sem=sum_send.at[2], recv_sem=sum_recv.at[2], device_id=partner, device_id_type=MESH,
    )
    swap.start()
    swap.wait()
    gram_out[...] = whole[...]
    save.wait()


def basis_kernel(gram_ref, block_ref, state_hbm, basis_ref, state_out, weight, sem):
    step = pl.program_id(0)
    move = pltpu.make_async_copy(state_hbm, state_out, sem)

    @pl.when(step == 0)
    def _():
        move.start()
        folded = jnp.concatenate([gram_ref[0], gram_ref[1]], axis=0)
        gram = jnp.concatenate([pltpu.roll(folded, 64, 1), folded], axis=0)
        row = lax.broadcasted_iota(jnp.int32, (MODES, TILE), 0)
        lane = lanes((MODES, TILE))
        work = jnp.where(lane < MODES, gram, jnp.where(lane == row + MODES, 1.0, 0.0))
        for k in range(MODES):
            start = (k // 8) * 8
            column = jnp.broadcast_to(work[start:, k : k + 1], (MODES - start, TILE))
            pivot_row = work[k : k + 1, :]
            scaled = pivot_row / column[k - start : k - start + 1, :]
            below = row[start:] > k
            changed = work[start:] - jnp.where(below, column * scaled, 0.0)
            work = jnp.concatenate([work[:start], changed], axis=0) if start else changed
        diagonal = jnp.sum(jnp.where(lane == row, work, 0.0), axis=1, keepdims=True)
        inverse = work[:, MODES:] * (1.0 / jnp.sqrt(diagonal))
        high = inverse.astype(jnp.bfloat16)
        rest = inverse - high.astype(jnp.float32)
        middle = rest.astype(jnp.bfloat16)
        low = (rest - middle.astype(jnp.float32)).astype(jnp.bfloat16)
        weight[...] = jnp.concatenate([high, middle, low], axis=1)

    for start in range(0, basis_ref.shape[1], 8):
        part = block_ref[:, start * TILE : (start + 8) * TILE]
        rows = jnp.dot(
            weight[...], jnp.concatenate([part, part, part], axis=0), preferred_element_type=jnp.float32
        )
        stacked = jnp.stack([rows[:, i * TILE : (i + 1) * TILE] for i in range(8)], axis=0)
        basis_ref[:, start : start + 8, :] = jnp.swapaxes(stacked, 0, 1)

    @pl.when(step == pl.num_programs(0) - 1)
    def _():
        move.wait()


def body(flow_state, sound_speed_sq, snapshots):
    anywhere = pl.BlockSpec(memory_space=pl.ANY)
    local = pl.BlockSpec(memory_space=pltpu.VMEM)
    field = (FIELDS, ROWS, TILE)
    f32, bf16 = jnp.float32, jnp.bfloat16
    new_state, block, gram = pl.pallas_call(
        wide_kernel,
        out_shape=(
            jax.ShapeDtypeStruct((4, TILE, TILE), f32),
            jax.ShapeDtypeStruct((MODES, TILE * TILE), bf16),
            jax.ShapeDtypeStruct((2, 16, TILE), f32),
        ),
        in_specs=[anywhere] * 3,
        out_specs=(local, anywhere, local),
        scratch_shapes=[
            pltpu.VMEM((MODES, TILE, TILE), bf16),
            pltpu.VMEM((MODES, TILE * TILE), bf16),
            pltpu.VMEM(field, f32),
            pltpu.VMEM(field, f32),
            pltpu.VMEM((4, ROWS, TILE), f32),
            pltpu.VMEM((4, ROWS, TILE), f32),
            pltpu.VMEM((4, ROWS, TILE), f32),
            pltpu.VMEM((4, ROWS, TILE), f32),
            pltpu.VMEM((TILE, TILE), f32),
            pltpu.VMEM((ROWS, TILE), f32),
            pltpu.VMEM((ROWS, TILE), f32),
            pltpu.VMEM((2, 16, TILE), f32),
            pltpu.VMEM((GY - 1, 16, TILE), f32),
            pltpu.VMEM((GX - 1, 16, TILE), f32),
            pltpu.VMEM((16, TILE), f32),
            pltpu.VMEM((2, 16, TILE), f32),
            pltpu.SemaphoreType.DMA((3,)),
            pltpu.SemaphoreType.DMA((8,)),
            pltpu.SemaphoreType.DMA((8,)),
            pltpu.SemaphoreType.DMA((3,)),
            pltpu.SemaphoreType.DMA((3,)),
        ],
        compiler_params=pltpu.CompilerParams(
            collective_id=0, has_side_effects=True, vmem_limit_bytes=40 << 20
        ),
        name="flow_and_gram",
    )(flow_state, sound_speed_sq, snapshots)

    rows = 32
    pod_basis, new_state = pl.pallas_call(
        basis_kernel,
        grid=(TILE // rows,),
        out_shape=(
            jax.ShapeDtypeStruct((MODES, TILE, TILE), f32),
            jax.ShapeDtypeStruct((4, TILE, TILE), f32),
        ),
        in_specs=[
            pl.BlockSpec((2, 16, TILE), lambda i: (0, 0, 0)),
            pl.BlockSpec((MODES, rows * TILE), lambda i: (0, i)),
            anywhere,
        ],
        out_specs=(pl.BlockSpec((MODES, rows, TILE), lambda i: (0, i, 0)), anywhere),
        scratch_shapes=[pltpu.VMEM((MODES, 3 * MODES), bf16), pltpu.SemaphoreType.DMA],
        compiler_params=pltpu.CompilerParams(vmem_limit_bytes=20 << 20),
        name="basis",
    )(gram, block, new_state)
    return new_state, pod_basis


def solution(mesh):
    placed = (P(None, "gx", "gy"), P("gx", "gy"), P(None, "gx", "gy"))
    return jax.shard_map(
        body,
        mesh=mesh,
        in_specs=placed,
        out_specs=(P(None, "gx", "gy"), P(None, "gx", "gy")),
        check_vma=False,
    )
```

```python
import jax
import jax.numpy as jnp
from jax import lax
from jax.experimental import pallas as pl
from jax.experimental.pallas import tpu as pltpu
from jax.sharding import PartitionSpec as P

MESH = pl.DeviceIdType.MESH
STEPS = 2
courant = 0.8
stream_speed = 0.3
span_speed = 0.1

MODES = 64
RESIDENT = 62
TILE = 128
HALO = 12
PAD = 16
ROWS = TILE + 2 * PAD
FIELDS = 5
GX = 32
GY = 8


def lanes(shape):
    return lax.broadcasted_iota(jnp.int32, shape, len(shape) - 1)


def slope_rows(ref, window, field, row, rows):
    near = ref[window, field, pl.ds(row + 1, rows), :] - ref[window, field, pl.ds(row - 1, rows), :]
    far = ref[window, field, pl.ds(row + 2, rows), :] - ref[window, field, pl.ds(row - 2, rows), :]
    return 8.0 * near - far


def slope_lanes(value):
    near = pltpu.roll(value, TILE - 1, 1) - pltpu.roll(value, 1, 1)
    far = pltpu.roll(value, TILE - 2, 1) - pltpu.roll(value, 2, 1)
    return 8.0 * near - far


def stage(kind, margin, state, source, target, sound):
    rows, scale = 8, courant / 12.0
    for row in range(PAD - margin, PAD + TILE + margin, rows):
        here = pl.ds(row, rows)
        for w in range(2):
            centre = [source[w, f, here, :] for f in range(4)]
            dx = [slope_rows(source, w, f, row, rows) for f in range(4)]
            dy = [slope_lanes(centre[f]) for f in range(4)]
            diverge = dx[1] + dy[2]
            advect = [stream_speed * dx[f] + span_speed * dy[f] for f in range(4)]
            rate = [
                advect[0] + diverge,
                advect[1] + dx[3],
                advect[2] + dy[3],
                advect[3] + sound[w, 4, here, :] * diverge,
            ]
            for f in range(4):
                if kind == 1:
                    moved = centre[f] - scale * rate[f]
                elif kind == 2:
                    moved = 0.75 * state[w, f, here, :] + (0.25 * centre[f] - (0.25 * scale) * rate[f])
                else:
                    moved = (1.0 / 3.0) * state[w, f, here, :] + (
                        (2.0 / 3.0) * centre[f] - (2.0 / 3.0 * scale) * rate[f]
                    )
                target[w, f, here, :] = moved


def joined(wide, field, row, rows):
    here = pl.ds(PAD + row, rows)
    lane = lanes((rows, TILE))
    first = (lane >= HALO) & (lane < 64)
    both = jnp.where(first, wide[0, field, here, :], wide[1, field, here, :])
    return pltpu.roll(both, TILE - HALO, 1)


def spread(row):
    return jnp.broadcast_to(row, (8, TILE))


def inverse_factor(gram):
    count = MODES // 8
    lane, sub = lanes((8, TILE)), lax.broadcasted_iota(jnp.int32, (8, TILE), 0)
    tiles = [
        jnp.where(lane < MODES, gram[8 * r : 8 * r + 8], jnp.where(lane == MODES + 8 * r + sub, 1.0, 0.0))
        for r in range(count)
    ]
    for t in range(count):
        column = {
            (j, r): jnp.broadcast_to(tiles[r][:, 8 * t + j : 8 * t + j + 1], (8, TILE))
            for j in range(8)
            for r in range(t, count)
        }
        for j in range(8):
            inverse_pivot = 1.0 / spread(column[j, t][j : j + 1, :])
            factor = {r: column[j, r] * inverse_pivot for r in range(t, count)}
            factor[t] = jnp.where(sub > j, factor[t], 0.0)
            for later in range(j + 1, 8):
                entry = spread(column[later, t][j : j + 1, :])
                for r in range(t, count):
                    column[later, r] = column[later, r] - factor[r] * entry
            pivot_row = spread(tiles[t][j : j + 1, :])
            for r in range(t, count):
                tiles[r] = tiles[r] - factor[r] * pivot_row
    rows = []
    for r in range(count):
        diagonal = jnp.sum(jnp.where(lane == 8 * r + sub, tiles[r], 0.0), axis=1, keepdims=True)
        scaled = pltpu.roll(tiles[r] * (1.0 / jnp.sqrt(diagonal)), MODES, 1)
        rows.append(jnp.where(lane < MODES, scaled, 0.0))
    return jnp.concatenate(rows, axis=0)


def exact_dot(a, b, contract):
    return lax.dot_general(
        a, b, (contract, ((), ())), precision=lax.Precision.HIGHEST, preferred_element_type=jnp.float32
    )


def turn(snap, block, group):
    modes = pl.ds(group * 16, 16)
    for row in range(0, TILE, 16):
        turned = jnp.swapaxes(snap[modes, row : row + 16, :], 0, 1)
        for i in range(16):
            block[modes, (row + i) * TILE : (row + i + 1) * TILE] = turned[i]


def wide_kernel(
    flow_hbm, sound_hbm, snap_hbm, state_out, block, inverse_out,
    snap, tile, wide, one, two, strip, left_strip, right_strip,
    packed, part_one, part_two, total_two, whole,
    late, late_one, late_two, late_total,
    load_sem, halo_send, halo_recv, sum_send, sum_recv,
):
    gx, gy = lax.axis_index("gx"), lax.axis_index("gy")
    core = lax.rem(gy, 2)
    cells = GX * GY * TILE * TILE

    def at(dx, dy):
        return (lax.rem(gx + (dx + GX), GX), lax.rem(gy + (dy + GY), GY))

    row_peers = [at(d, 0) for d in range(1, GX)]
    column_peers = [at(0, d) for d in range(1, GY)]
    corner_peers = [at(dx, dy) for dx in (-1, 1) for dy in (-1, 1)]
    everyone = row_peers + column_peers + corner_peers

    barrier = pltpu.get_barrier_semaphore()
    for peer in everyone:
        pl.semaphore_signal(barrier, inc=1, device_id=peer, device_id_type=MESH)

    inside = pl.ds(PAD, TILE)
    loads = [
        pltpu.make_async_copy(flow_hbm, tile.at[pl.ds(0, 4), inside, :], load_sem.at[0]),
        pltpu.make_async_copy(sound_hbm, tile.at[4, inside, :], load_sem.at[1]),
        pltpu.make_async_copy(snap_hbm, snap.at[pl.ds(0, RESIDENT)], load_sem.at[2]),
    ]
    for load in loads:
        load.start()
    snap[RESIDENT:MODES] = jnp.zeros((MODES - RESIDENT, TILE, TILE), jnp.bfloat16)
    loads[0].wait()
    loads[1].wait()

    lane = lanes((16, TILE))
    for row in range(0, TILE, 16):
        gathered = pltpu.roll(tile[0, pl.ds(PAD + row, 16), :], HALO, 1)
        for f in range(1, FIELDS):
            moved = pltpu.roll(tile[f, pl.ds(PAD + row, 16), :], HALO + 24 * f, 1)
            gathered = jnp.where(lane >= 24 * f, moved, gathered)
        strip[pl.ds(row, 16), :] = gathered

    loads[2].wait()
    for group in range(4):
        turn(snap, block, group)
    gram = lax.dot_general(
        block[...], block[...], (((1,), (1,)), ((), ())), preferred_element_type=jnp.float32
    ) * (1.0 / cells)
    folded = jnp.concatenate([gram[32:64], gram[0:32]], axis=1)
    packed[0] = folded[0:16]
    packed[1] = folded[16:32]

    pl.semaphore_wait(barrier, len(everyone))

    top, bottom = pl.ds(0, PAD), pl.ds(PAD + TILE, PAD)
    low, high = pl.ds(0, PAD), pl.ds(TILE - PAD, PAD)
    moves = [
        (tile.at[:, pl.ds(TILE, PAD), :], tile.at[:, top, :], at(1, 0)),
        (tile.at[:, pl.ds(PAD, PAD), :], tile.at[:, bottom, :], at(-1, 0)),
        (strip, left_strip.at[inside, :], at(0, 1)),
        (strip, right_strip.at[inside, :], at(0, -1)),
        (strip.at[high, :], left_strip.at[top, :], at(1, 1)),
        (strip.at[low, :], left_strip.at[bottom, :], at(-1, 1)),
        (strip.at[high, :], right_strip.at[top, :], at(1, -1)),
        (strip.at[low, :], right_strip.at[bottom, :], at(-1, -1)),
    ]
    halos = []
    for number, (source, target, peer) in enumerate(moves):
        halos.append(
            pltpu.make_async_remote_copy(
                src_ref=source, dst_ref=target, send_sem=halo_send.at[number],
                recv_sem=halo_recv.at[number], device_id=peer, device_id_type=MESH,
            )
        )
        halos[-1].start()

    def send(source, target, slot, peer):
        copy = pltpu.make_async_remote_copy(
            src_ref=source, dst_ref=target, send_sem=sum_send.at[slot],
            recv_sem=sum_recv.at[slot], device_id=peer, device_id_type=MESH,
        )
        copy.start()
        return copy

    def received(ref, slot):
        pltpu.make_async_copy(ref, ref, sum_recv.at[slot]).wait()

    def sent(ref, slot):
        pltpu.make_async_copy(ref, ref, sum_send.at[slot]).wait()

    for number, peer in enumerate(column_peers):
        send(packed.at[lax.rem(peer[1], 2)], part_one.at[number], 0, peer)

    for halo in halos:
        halo.wait()
    for row in range(0, ROWS, 16):
        here = pl.ds(row, 16)
        merged = jnp.where(lax.rem(lane, 24) >= HALO, right_strip[here, :], left_strip[here, :])
        for f in range(FIELDS):
            beside = pltpu.roll(merged, TILE - 24 * f, 1) if f else merged
            turned = pltpu.roll(tile[f, here, :], HALO, 1)
            wide[0, f, here, :] = jnp.where(lane < HALO, beside, turned)
            wide[1, f, here, :] = jnp.where((lane >= HALO) & (lane < 2 * HALO), beside, turned)

    stage(1, 10, wide, wide, one, wide)

    received(part_one, 0)
    total = packed[core]
    for number in range(GY - 1):
        total = total + part_one[number]
    total_two[...] = total
    for number, peer in enumerate(row_peers):
        send(total_two, part_two.at[number], 1, peer)

    stage(2, 8, wide, one, two, wide)
    stage(3, 6, wide, two, wide, wide)
    snap[RESIDENT] = joined(wide, 3, 0, TILE).astype(jnp.bfloat16)
    stage(1, 4, wide, wide, one, wide)
    stage(2, 2, wide, one, two, wide)
    stage(3, 0, wide, two, wide, wide)
    snap[RESIDENT + 1] = joined(wide, 3, 0, TILE).astype(jnp.bfloat16)

    turn(snap, block, 3)
    fresh = lax.dot_general(
        block[48:64, :], block[...], (((1,), (1,)), ((), ())), preferred_element_type=jnp.float32
    ) * (1.0 / cells)
    late[...] = jnp.concatenate([fresh[14:15], fresh[15:16]], axis=1)
    for number, peer in enumerate(column_peers):
        send(late, late_one.at[number], 3, peer)

    for f in range(4):
        state_out[f] = joined(wide, f, 0, TILE)

    received(part_two, 1)
    total = total_two[...]
    for number in range(GX - 1):
        total = total + part_two[number]
    whole[core] = total
    partner = (gx, gy + 1 - 2 * core)
    swap = send(whole.at[core], whole.at[core], 2, partner)

    received(late_one, 3)
    late_total[...] = late[...] + jnp.sum(late_one[...], axis=0)
    for number, peer in enumerate(row_peers):
        send(late_total, late_two.at[number], 4, peer)

    swap.wait()
    folded = jnp.concatenate([whole[0], whole[1]], axis=0)
    gram = jnp.concatenate([pltpu.roll(folded, MODES, 1), folded], axis=0)
    row = lax.broadcasted_iota(jnp.int32, (MODES, TILE), 0)
    unit = (row >= RESIDENT) & (row == lanes((MODES, TILE)))
    early = inverse_factor(jnp.where(unit, 1.0, gram))
    inverse_out[...] = early

    received(late_two, 4)
    pair = late_total[...] + jnp.sum(late_two[...], axis=0)
    lane = lanes((1, TILE))
    first = jnp.where(lane < MODES, pair, 0.0)
    second = jnp.where(lane < MODES, pltpu.roll(pair, MODES, 1), 0.0)

    def pick(vector, place):
        return jnp.sum(jnp.where(lane == place, vector, 0.0), axis=1, keepdims=True)

    norm_first, norm_second, cross = pick(first, 62), pick(second, 63), pick(second, 62)
    known = lane < RESIDENT
    both = jnp.concatenate(
        [jnp.where(known, first, 0.0), jnp.where(known, second, 0.0), jnp.zeros((6, TILE), jnp.float32)], axis=0
    )
    along = exact_dot(both, early, ((1,), (1,)))
    back = exact_dot(along, early, ((1,), (0,)))
    along_first, along_second = along[0:1], along[1:2]
    scale_first = 1.0 / jnp.sqrt(norm_first - jnp.sum(along_first * along_first, axis=1, keepdims=True))
    row_first = (jnp.where(lane == 62, 1.0, 0.0) - back[0:1]) * scale_first
    shared = (cross - jnp.sum(along_first * along_second, axis=1, keepdims=True)) * scale_first
    left = norm_second - jnp.sum(along_second * along_second, axis=1, keepdims=True) - shared * shared
    row_second = (jnp.where(lane == 63, 1.0, 0.0) - back[1:2] - shared * row_first) * (1.0 / jnp.sqrt(left))
    inverse_out[62:63, :] = row_first
    inverse_out[63:64, :] = row_second

    sent(part_one, 0)
    sent(part_two, 1)
    sent(late_one, 3)
    sent(late_two, 4)


def basis_kernel(inverse_ref, block_ref, state_hbm, basis_hbm, state_out, basis, sem, state_sem):
    move = pltpu.make_async_copy(state_hbm, state_out, state_sem)
    move.start()
    inverse = inverse_ref[:, :MODES]
    high = inverse.astype(jnp.bfloat16)
    rest = inverse - high.astype(jnp.float32)
    middle = rest.astype(jnp.bfloat16)
    low = (rest - middle.astype(jnp.float32)).astype(jnp.bfloat16)
    weight = jnp.concatenate([high, middle, low], axis=1)
    copies = []
    for start in range(0, TILE, 8):
        part = block_ref[:, start * TILE : (start + 8) * TILE]
        rows = jnp.dot(weight, jnp.concatenate([part, part, part], axis=0), preferred_element_type=jnp.float32)
        stacked = jnp.stack([rows[:, i * TILE : (i + 1) * TILE] for i in range(8)], axis=0)
        here = pl.ds(start, 8)
        basis[:, here, :] = jnp.swapaxes(stacked, 0, 1)
        copies.append(pltpu.make_async_copy(basis.at[:, here, :], basis_hbm.at[:, here, :], sem.at[start // 8]))
        copies[-1].start()
    for copy in copies:
        copy.wait()
    move.wait()


def first(flow_state, sound_speed_sq, snapshots):
    hbm = pl.BlockSpec(memory_space=pltpu.HBM)
    local = pl.BlockSpec(memory_space=pltpu.VMEM)
    f32, bf16 = jnp.float32, jnp.bfloat16
    wide = pltpu.VMEM((2, 4, ROWS, TILE), f32)
    return pl.pallas_call(
        wide_kernel,
        out_shape=(
            jax.ShapeDtypeStruct((4, TILE, TILE), f32),
            jax.ShapeDtypeStruct((MODES, TILE * TILE), bf16),
            jax.ShapeDtypeStruct((MODES, TILE), f32),
        ),
        in_specs=[hbm] * 3,
        out_specs=(local, local, local),
        scratch_shapes=[
            pltpu.VMEM((MODES, TILE, TILE), bf16),
            pltpu.VMEM((FIELDS, ROWS, TILE), f32),
            pltpu.VMEM((2, FIELDS, ROWS, TILE), f32),
            wide,
            wide,
            pltpu.VMEM((TILE, TILE), f32),
            pltpu.VMEM((ROWS, TILE), f32),
            pltpu.VMEM((ROWS, TILE), f32),
            pltpu.VMEM((2, 16, TILE), f32),
            pltpu.VMEM((GY - 1, 16, TILE), f32),
            pltpu.VMEM((GX - 1, 16, TILE), f32),
            pltpu.VMEM((16, TILE), f32),
            pltpu.VMEM((2, 16, TILE), f32),
            pltpu.VMEM((1, TILE), f32),
            pltpu.VMEM((GY - 1, 1, TILE), f32),
            pltpu.VMEM((GX - 1, 1, TILE), f32),
            pltpu.VMEM((1, TILE), f32),
            pltpu.SemaphoreType.DMA((3,)),
            pltpu.SemaphoreType.DMA((8,)),
            pltpu.SemaphoreType.DMA((8,)),
            pltpu.SemaphoreType.DMA((5,)),
            pltpu.SemaphoreType.DMA((5,)),
        ],
        compiler_params=pltpu.CompilerParams(
            collective_id=0, has_side_effects=True, vmem_limit_bytes=40 << 20
        ),
        name="flow_and_gram",
    )(*(pltpu.with_memory_space_constraint(x, pltpu.HBM) for x in (flow_state, sound_speed_sq, snapshots)))


def body(flow_state, sound_speed_sq, snapshots):
    new_state, block, inverse = first(flow_state, sound_speed_sq, snapshots)
    local = pl.BlockSpec(memory_space=pltpu.VMEM)
    anywhere = pl.BlockSpec(memory_space=pl.ANY)
    hbm = pl.BlockSpec(memory_space=pltpu.HBM)
    f32 = jnp.float32
    pod_basis, new_state = pl.pallas_call(
        basis_kernel,
        out_shape=(
            jax.ShapeDtypeStruct((MODES, TILE, TILE), f32),
            jax.ShapeDtypeStruct((4, TILE, TILE), f32),
        ),
        in_specs=[local, local, anywhere],
        out_specs=(hbm, hbm),
        scratch_shapes=[
            pltpu.VMEM((MODES, TILE, TILE), f32),
            pltpu.SemaphoreType.DMA((TILE // 8,)),
            pltpu.SemaphoreType.DMA,
        ],
        compiler_params=pltpu.CompilerParams(vmem_limit_bytes=20 << 20),
        name="basis",
    )(inverse, block, new_state)
    return new_state, pod_basis


def solution(mesh):
    placed = (P(None, "gx", "gy"), P("gx", "gy"), P(None, "gx", "gy"))
    return jax.shard_map(
        body,
        mesh=mesh,
        in_specs=placed,
        out_specs=(P(None, "gx", "gy"), P(None, "gx", "gy")),
        check_vma=False,
    )
```

```python
import jax
import jax.numpy as jnp
from jax import lax
from jax.experimental import pallas as pl
from jax.experimental.pallas import tpu as pltpu
from jax.sharding import PartitionSpec as P

MESH = pl.DeviceIdType.MESH
STEPS = 2
courant = 0.8
stream_speed = 0.3
span_speed = 0.1

MODES = 64
RESIDENT = 62
TILE = 128
HALO = 12
PAD = 16
ROWS = TILE + 2 * PAD
FIELDS = 5
GX = 32
GY = 8


def lanes(shape):
    return lax.broadcasted_iota(jnp.int32, shape, len(shape) - 1)


def slope_rows(ref, window, field, row, rows):
    near = ref[window, field, pl.ds(row + 1, rows), :] - ref[window, field, pl.ds(row - 1, rows), :]
    far = ref[window, field, pl.ds(row + 2, rows), :] - ref[window, field, pl.ds(row - 2, rows), :]
    return 8.0 * near - far


def slope_lanes(value):
    near = pltpu.roll(value, TILE - 1, 1) - pltpu.roll(value, 1, 1)
    far = pltpu.roll(value, TILE - 2, 1) - pltpu.roll(value, 2, 1)
    return 8.0 * near - far


def lane_band():
    away = lax.rem(
        lax.broadcasted_iota(jnp.int32, (TILE, TILE), 0) - lanes((TILE, TILE)) + TILE, TILE
    )
    band = jnp.where(away == 1, 8.0, jnp.where(away == TILE - 1, -8.0, 0.0))
    band = jnp.where(away == 2, -1.0, jnp.where(away == TILE - 2, 1.0, band)).astype(jnp.bfloat16)
    return jnp.concatenate([band, band, band], axis=0)


def split(value):
    high = value.astype(jnp.bfloat16)
    rest = value - high.astype(jnp.float32)
    middle = rest.astype(jnp.bfloat16)
    return [high, middle, (rest - middle.astype(jnp.float32)).astype(jnp.bfloat16)]


def stage(kind, margin, state, source, target, sound, band):
    scale = courant / 12.0
    row, end = PAD - margin, PAD + TILE + margin
    while row < end:
        rows = 16 if end - row > 8 else 8
        here = pl.ds(row, rows)
        for w in range(2):
            centre = [source[w, f, here, :] for f in range(4)]
            dx = [slope_rows(source, w, f, row, rows) for f in range(4)]
            pair = jnp.concatenate(split(jnp.concatenate(centre[2:], axis=0)), axis=1)
            pair = jnp.dot(pair, band, preferred_element_type=jnp.float32)
            dy = [slope_lanes(centre[0]), slope_lanes(centre[1]), pair[:rows], pair[rows:]]
            diverge = dx[1] + dy[2]
            advect = [stream_speed * dx[f] + span_speed * dy[f] for f in range(4)]
            rate = [
                advect[0] + diverge,
                advect[1] + dx[3],
                advect[2] + dy[3],
                advect[3] + sound[w, 4, here, :] * diverge,
            ]
            for f in range(4):
                if kind == 1:
                    moved = centre[f] - scale * rate[f]
                elif kind == 2:
                    moved = 0.75 * state[w, f, here, :] + (0.25 * centre[f] - (0.25 * scale) * rate[f])
                else:
                    moved = (1.0 / 3.0) * state[w, f, here, :] + (
                        (2.0 / 3.0) * centre[f] - (2.0 / 3.0 * scale) * rate[f]
                    )
                target[w, f, here, :] = moved
        row += rows


def joined(wide, field, row, rows):
    here = pl.ds(PAD + row, rows)
    lane = lanes((rows, TILE))
    first = (lane >= HALO) & (lane < 64)
    both = jnp.where(first, wide[0, field, here, :], wide[1, field, here, :])
    return pltpu.roll(both, TILE - HALO, 1)


def spread(row):
    return jnp.broadcast_to(row, (8, TILE))


def inverse_factor(gram):
    count = MODES // 8
    lane, sub = lanes((8, TILE)), lax.broadcasted_iota(jnp.int32, (8, TILE), 0)
    tiles = [
        jnp.where(lane < MODES, gram[8 * r : 8 * r + 8], jnp.where(lane == MODES + 8 * r + sub, 1.0, 0.0))
        for r in range(count)
    ]
    for t in range(count):
        column = {
            (j, r): jnp.broadcast_to(tiles[r][:, 8 * t + j : 8 * t + j + 1], (8, TILE))
            for j in range(8)
            for r in range(t, count)
        }
        for j in range(8):
            inverse_pivot = 1.0 / spread(column[j, t][j : j + 1, :])
            factor = {r: column[j, r] * inverse_pivot for r in range(t, count)}
            factor[t] = jnp.where(sub > j, factor[t], 0.0)
            for later in range(j + 1, 8):
                entry = spread(column[later, t][j : j + 1, :])
                for r in range(t, count):
                    column[later, r] = column[later, r] - factor[r] * entry
            pivot_row = spread(tiles[t][j : j + 1, :])
            for r in range(t, count):
                tiles[r] = tiles[r] - factor[r] * pivot_row
    rows = []
    for r in range(count):
        diagonal = jnp.sum(jnp.where(lane == 8 * r + sub, tiles[r], 0.0), axis=1, keepdims=True)
        scaled = pltpu.roll(tiles[r] * (1.0 / jnp.sqrt(diagonal)), MODES, 1)
        rows.append(jnp.where(lane < MODES, scaled, 0.0))
    return jnp.concatenate(rows, axis=0)


def exact_dot(a, b, contract):
    return lax.dot_general(
        a, b, (contract, ((), ())), precision=lax.Precision.HIGHEST, preferred_element_type=jnp.float32
    )


def turn(snap, block, group):
    modes = pl.ds(group * 16, 16)
    for row in range(0, TILE, 16):
        turned = jnp.swapaxes(snap[modes, row : row + 16, :], 0, 1)
        for i in range(16):
            block[modes, (row + i) * TILE : (row + i + 1) * TILE] = turned[i]


def wide_kernel(
    flow_hbm, sound_hbm, snap_hbm, state_out, block, inverse_out,
    snap, tile, wide, one, two, strip, left_strip, right_strip,
    packed, part_one, part_two, total_two, whole,
    line, late, late_one, late_two, late_total,
    reach_sem, load_sem, halo_send, halo_recv, sum_send, sum_recv,
):
    gx, gy = lax.axis_index("gx"), lax.axis_index("gy")
    core = lax.rem(gy, 2)
    cells = GX * GY * TILE * TILE

    def at(dx, dy):
        return (lax.rem(gx + (dx + GX), GX), lax.rem(gy + (dy + GY), GY))

    x, z, y = gx // 8, lax.rem(gx, 8), gy // 2
    row_steps = sorted(
        ((dx, dz) for dx in range(4) for dz in range(8) if dx or dz),
        key=lambda step: -min(step[0], 4 - step[0]) - min(step[1], 8 - step[1]),
    )
    row_peers = [(lax.rem(x + dx, 4) * 8 + lax.rem(z + dz, 8), gy) for dx, dz in row_steps]
    column_steps = sorted(
        ((dy, dc) for dy in range(4) for dc in range(2) if dy or dc), key=lambda step: -min(step[0], 4 - step[0])
    )
    column_peers = [(gx, lax.rem(y + dy, 4) * 2 + lax.rem(core + dc, 2)) for dy, dc in column_steps]
    corner_peers = [at(dx, dy) for dx in (-1, 1) for dy in (-1, 1)]
    near_peers = [
        peer
        for (dx, dz), peer in zip(row_steps, row_peers)
        if min(dx, 4 - dx) <= 1 and min(dz, 8 - dz) <= 2
    ]
    entered = near_peers + column_peers + corner_peers

    barrier = pltpu.get_barrier_semaphore()
    for peer in entered:
        pl.semaphore_signal(barrier, inc=1, device_id=peer, device_id_type=MESH)

    inside = pl.ds(PAD, TILE)
    loads = [
        pltpu.make_async_copy(flow_hbm, tile.at[pl.ds(0, 4), inside, :], load_sem.at[0]),
        pltpu.make_async_copy(sound_hbm, tile.at[4, inside, :], load_sem.at[1]),
        pltpu.make_async_copy(snap_hbm, snap.at[pl.ds(0, RESIDENT)], load_sem.at[2]),
    ]
    for load in loads:
        load.start()
    line[...] = jnp.zeros((TILE, 8, TILE), jnp.float32)
    snap[RESIDENT:MODES] = jnp.zeros((MODES - RESIDENT, TILE, TILE), jnp.bfloat16)
    loads[0].wait()
    loads[1].wait()

    lane = lanes((16, TILE))
    for row in range(0, TILE, 16):
        gathered = pltpu.roll(tile[0, pl.ds(PAD + row, 16), :], HALO, 1)
        for f in range(1, FIELDS):
            moved = pltpu.roll(tile[f, pl.ds(PAD + row, 16), :], HALO + 24 * f, 1)
            gathered = jnp.where(lane >= 24 * f, moved, gathered)
        strip[pl.ds(row, 16), :] = gathered

    loads[2].wait()
    for group in range(4):
        turn(snap, block, group)
    pl.semaphore_wait(barrier, len(entered))

    top, bottom = pl.ds(0, PAD), pl.ds(PAD + TILE, PAD)
    low, high = pl.ds(0, PAD), pl.ds(TILE - PAD, PAD)
    moves = [
        (tile.at[:, pl.ds(TILE, PAD), :], tile.at[:, top, :], at(1, 0)),
        (tile.at[:, pl.ds(PAD, PAD), :], tile.at[:, bottom, :], at(-1, 0)),
        (strip, left_strip.at[inside, :], at(0, 1)),
        (strip, right_strip.at[inside, :], at(0, -1)),
        (strip.at[high, :], left_strip.at[top, :], at(1, 1)),
        (strip.at[low, :], left_strip.at[bottom, :], at(-1, 1)),
        (strip.at[high, :], right_strip.at[top, :], at(1, -1)),
        (strip.at[low, :], right_strip.at[bottom, :], at(-1, -1)),
    ]
    halos = []
    for number, (source, target, peer) in enumerate(moves):
        halos.append(
            pltpu.make_async_remote_copy(
                src_ref=source, dst_ref=target, send_sem=halo_send.at[number],
                recv_sem=halo_recv.at[number], device_id=peer, device_id_type=MESH,
            )
        )
        halos[-1].start()

    def send(source, target, slot, peer):
        copy = pltpu.make_async_remote_copy(
            src_ref=source, dst_ref=target, send_sem=sum_send.at[slot],
            recv_sem=sum_recv.at[slot], device_id=peer, device_id_type=MESH,
        )
        copy.start()
        return copy

    def received(ref, slot):
        pltpu.make_async_copy(ref, ref, sum_recv.at[slot]).wait()

    def sent(ref, slot):
        pltpu.make_async_copy(ref, ref, sum_send.at[slot]).wait()

    for peer in near_peers:
        pl.semaphore_signal(reach_sem, inc=1, device_id=peer, device_id_type=MESH)

    gram = lax.dot_general(
        block[...], block[...], (((1,), (1,)), ((), ())), preferred_element_type=jnp.float32
    ) * (1.0 / cells)
    folded = jnp.concatenate([gram[32:64], gram[0:32]], axis=1)
    packed[0] = folded[0:16]
    packed[1] = folded[16:32]

    for number, peer in enumerate(column_peers):
        send(packed.at[lax.rem(peer[1], 2)], part_one.at[number], 0, peer)

    for halo in halos:
        halo.wait()
    for row in range(0, ROWS, 16):
        here = pl.ds(row, 16)
        merged = jnp.where(lax.rem(lane, 24) >= HALO, right_strip[here, :], left_strip[here, :])
        for f in range(FIELDS):
            beside = pltpu.roll(merged, TILE - 24 * f, 1) if f else merged
            turned = pltpu.roll(tile[f, here, :], HALO, 1)
            wide[0, f, here, :] = jnp.where(lane < HALO, beside, turned)
            wide[1, f, here, :] = jnp.where((lane >= HALO) & (lane < 2 * HALO), beside, turned)

    band = lane_band()
    stage(1, 10, wide, wide, one, wide, band)

    received(part_one, 0)
    total = packed[core]
    for number in range(GY - 1):
        total = total + part_one[number]
    total_two[...] = total
    pl.semaphore_wait(reach_sem, len(near_peers))
    for number, peer in enumerate(row_peers):
        send(total_two, part_two.at[number], 1, peer)

    stage(2, 8, wide, one, two, wide, band)
    stage(3, 6, wide, two, wide, wide, band)
    pressures = [joined(wide, 3, 0, TILE).astype(jnp.bfloat16)]
    snap[RESIDENT] = pressures[0]
    pressures[0] = pressures[0].astype(jnp.float32)
    line[:, 0, :] = pressures[0]
    stage(1, 4, wide, wide, one, wide, band)
    stage(2, 2, wide, one, two, wide, band)
    stage(3, 0, wide, two, wide, wide, band)
    pressures.append(joined(wide, 3, 0, TILE).astype(jnp.bfloat16))
    snap[RESIDENT + 1] = pressures[1]
    pressures[1] = pressures[1].astype(jnp.float32)
    line[:, 1, :] = pressures[1]

    flat = jnp.concatenate([line[i].astype(jnp.bfloat16) for i in range(TILE)], axis=1)
    fresh = lax.dot_general(flat, block[...], (((1,), (1,)), ((), ())), preferred_element_type=jnp.float32)

    def product(a, b):
        return jnp.sum(jnp.sum(pressures[a] * pressures[b], axis=0, keepdims=True), axis=1, keepdims=True)

    pair = jnp.concatenate([fresh[0:1], fresh[1:2]], axis=1)
    place = lanes((1, TILE))
    for where, value in ((62, product(0, 0)), (126, product(0, 1)), (127, product(1, 1))):
        pair = jnp.where(place == where, value, pair)
    late[...] = pair * (1.0 / cells)
    for number, peer in enumerate(column_peers):
        send(late, late_one.at[number], 3, peer)

    turn(snap, block, 3)

    for f in range(4):
        state_out[f] = joined(wide, f, 0, TILE)

    received(late_one, 3)
    late_total[...] = late[...] + jnp.sum(late_one[...], axis=0)
    for number, peer in enumerate(row_peers):
        send(late_total, late_two.at[number], 4, peer)

    received(part_two, 1)
    total = total_two[...]
    for number in range(GX - 1):
        total = total + part_two[number]
    whole[core] = total
    partner = (gx, gy + 1 - 2 * core)
    swap = send(whole.at[core], whole.at[core], 2, partner)

    swap.wait()
    folded = jnp.concatenate([whole[0], whole[1]], axis=0)
    gram = jnp.concatenate([pltpu.roll(folded, MODES, 1), folded], axis=0)
    row = lax.broadcasted_iota(jnp.int32, (MODES, TILE), 0)
    unit = (row >= RESIDENT) & (row == lanes((MODES, TILE)))
    early = inverse_factor(jnp.where(unit, 1.0, gram))
    inverse_out[...] = early
    normal = exact_dot(early, early, ((0,), (0,)))

    received(late_two, 4)
    pair = late_total[...] + jnp.sum(late_two[...], axis=0)
    lane = lanes((1, TILE))
    first = jnp.where(lane < MODES, pair, 0.0)
    second = jnp.where(lane < MODES, pltpu.roll(pair, MODES, 1), 0.0)

    def pick(vector, place):
        return jnp.sum(jnp.where(lane == place, vector, 0.0), axis=1, keepdims=True)

    norm_first, norm_second, cross = pick(first, 62), pick(second, 63), pick(second, 62)
    known = lane < RESIDENT
    both = jnp.concatenate(
        [jnp.where(known, first, 0.0), jnp.where(known, second, 0.0), jnp.zeros((6, TILE), jnp.float32)], axis=0
    )
    along = exact_dot(both, early, ((1,), (1,)))
    back = exact_dot(both, normal, ((1,), (0,)))
    along_first, along_second = along[0:1], along[1:2]
    scale_first = 1.0 / jnp.sqrt(norm_first - jnp.sum(along_first * along_first, axis=1, keepdims=True))
    row_first = (jnp.where(lane == 62, 1.0, 0.0) - back[0:1]) * scale_first
    shared = (cross - jnp.sum(along_first * along_second, axis=1, keepdims=True)) * scale_first
    left = norm_second - jnp.sum(along_second * along_second, axis=1, keepdims=True) - shared * shared
    row_second = (jnp.where(lane == 63, 1.0, 0.0) - back[1:2] - shared * row_first) * (1.0 / jnp.sqrt(left))
    inverse_out[62:63, :] = row_first
    inverse_out[63:64, :] = row_second

    sent(part_one, 0)
    sent(part_two, 1)
    sent(late_one, 3)
    sent(late_two, 4)


def basis_kernel(inverse_ref, block_ref, state_hbm, basis_hbm, state_out, basis, sem, state_sem):
    move = pltpu.make_async_copy(state_hbm, state_out, state_sem)
    move.start()
    inverse = inverse_ref[:, :MODES]
    high = inverse.astype(jnp.bfloat16)
    rest = inverse - high.astype(jnp.float32)
    middle = rest.astype(jnp.bfloat16)
    low = (rest - middle.astype(jnp.float32)).astype(jnp.bfloat16)
    weight = jnp.concatenate([high, middle, low], axis=1)
    copies = []
    for start in range(0, TILE, 8):
        part = block_ref[:, start * TILE : (start + 8) * TILE]
        rows = jnp.dot(weight, jnp.concatenate([part, part, part], axis=0), preferred_element_type=jnp.float32)
        stacked = jnp.stack([rows[:, i * TILE : (i + 1) * TILE] for i in range(8)], axis=0)
        here = pl.ds(start, 8)
        basis[:, here, :] = jnp.swapaxes(stacked, 0, 1)
        copies.append(pltpu.make_async_copy(basis.at[:, here, :], basis_hbm.at[:, here, :], sem.at[start // 8]))
        copies[-1].start()
    for copy in copies:
        copy.wait()
    move.wait()


def first(flow_state, sound_speed_sq, snapshots):
    hbm = pl.BlockSpec(memory_space=pltpu.HBM)
    local = pl.BlockSpec(memory_space=pltpu.VMEM)
    f32, bf16 = jnp.float32, jnp.bfloat16
    wide = pltpu.VMEM((2, 4, ROWS, TILE), f32)
    return pl.pallas_call(
        wide_kernel,
        out_shape=(
            jax.ShapeDtypeStruct((4, TILE, TILE), f32),
            jax.ShapeDtypeStruct((MODES, TILE * TILE), bf16),
            jax.ShapeDtypeStruct((MODES, TILE), f32),
        ),
        in_specs=[hbm] * 3,
        out_specs=(local, local, local),
        scratch_shapes=[
            pltpu.VMEM((MODES, TILE, TILE), bf16),
            pltpu.VMEM((FIELDS, ROWS, TILE), f32),
            pltpu.VMEM((2, FIELDS, ROWS, TILE), f32),
            wide,
            wide,
            pltpu.VMEM((TILE, TILE), f32),
            pltpu.VMEM((ROWS, TILE), f32),
            pltpu.VMEM((ROWS, TILE), f32),
            pltpu.VMEM((2, 16, TILE), f32),
            pltpu.VMEM((GY - 1, 16, TILE), f32),
            pltpu.VMEM((GX - 1, 16, TILE), f32),
            pltpu.VMEM((16, TILE), f32),
            pltpu.VMEM((2, 16, TILE), f32),
            pltpu.VMEM((TILE, 8, TILE), f32),
            pltpu.VMEM((1, TILE), f32),
            pltpu.VMEM((GY - 1, 1, TILE), f32),
            pltpu.VMEM((GX - 1, 1, TILE), f32),
            pltpu.VMEM((1, TILE), f32),
            pltpu.SemaphoreType.REGULAR,
            pltpu.SemaphoreType.DMA((3,)),
            pltpu.SemaphoreType.DMA((8,)),
            pltpu.SemaphoreType.DMA((8,)),
            pltpu.SemaphoreType.DMA((5,)),
            pltpu.SemaphoreType.DMA((5,)),
        ],
        compiler_params=pltpu.CompilerParams(
            collective_id=0, has_side_effects=True, vmem_limit_bytes=40 << 20
        ),
        name="flow_and_gram",
    )(*(pltpu.with_memory_space_constraint(x, pltpu.HBM) for x in (flow_state, sound_speed_sq, snapshots)))


def body(flow_state, sound_speed_sq, snapshots):
    new_state, block, inverse = first(flow_state, sound_speed_sq, snapshots)
    local = pl.BlockSpec(memory_space=pltpu.VMEM)
    anywhere = pl.BlockSpec(memory_space=pl.ANY)
    hbm = pl.BlockSpec(memory_space=pltpu.HBM)
    f32 = jnp.float32
    pod_basis, new_state = pl.pallas_call(
        basis_kernel,
        out_shape=(
            jax.ShapeDtypeStruct((MODES, TILE, TILE), f32),
            jax.ShapeDtypeStruct((4, TILE, TILE), f32),
        ),
        in_specs=[local, local, anywhere],
        out_specs=(hbm, hbm),
        scratch_shapes=[
            pltpu.VMEM((MODES, TILE, TILE), f32),
            pltpu.SemaphoreType.DMA((TILE // 8,)),
            pltpu.SemaphoreType.DMA,
        ],
        compiler_params=pltpu.CompilerParams(vmem_limit_bytes=20 << 20),
        name="basis",
    )(inverse, block, new_state)
    return new_state, pod_basis


def solution(mesh):
    placed = (P(None, "gx", "gy"), P("gx", "gy"), P(None, "gx", "gy"))
    return jax.shard_map(
        body,
        mesh=mesh,
        in_specs=placed,
        out_specs=(P(None, "gx", "gy"), P(None, "gx", "gy")),
        check_vma=False,
    )
```

```python
import jax
import jax.numpy as jnp
from jax import lax
from jax.experimental import pallas as pl
from jax.experimental.pallas import tpu as pltpu
from jax.sharding import PartitionSpec as P

MESH = pl.DeviceIdType.MESH
STEPS = 2
courant = 0.8
stream_speed = 0.3
span_speed = 0.1

MODES = 64
RESIDENT = 62
TILE = 128
EARLY_ROWS = 64
HALO = 12
PAD = 16
ROWS = TILE + 2 * PAD
FIELDS = 5
GX = 32
GY = 8


def lanes(shape):
    return lax.broadcasted_iota(jnp.int32, shape, len(shape) - 1)


def slope_rows(ref, window, field, row, rows):
    near = ref[window, field, pl.ds(row + 1, rows), :] - ref[window, field, pl.ds(row - 1, rows), :]
    far = ref[window, field, pl.ds(row + 2, rows), :] - ref[window, field, pl.ds(row - 2, rows), :]
    return 8.0 * near - far


def slope_lanes(value):
    near = pltpu.roll(value, TILE - 1, 1) - pltpu.roll(value, 1, 1)
    far = pltpu.roll(value, TILE - 2, 1) - pltpu.roll(value, 2, 1)
    return 8.0 * near - far


def lane_band():
    away = lax.rem(
        lax.broadcasted_iota(jnp.int32, (TILE, TILE), 0) - lanes((TILE, TILE)) + TILE, TILE
    )
    band = jnp.where(away == 1, 8.0, jnp.where(away == TILE - 1, -8.0, 0.0))
    band = jnp.where(away == 2, -1.0, jnp.where(away == TILE - 2, 1.0, band)).astype(jnp.bfloat16)
    return jnp.concatenate([band, band, band], axis=0)


def split(value):
    high = value.astype(jnp.bfloat16)
    rest = value - high.astype(jnp.float32)
    middle = rest.astype(jnp.bfloat16)
    return [high, middle, (rest - middle.astype(jnp.float32)).astype(jnp.bfloat16)]


def stage(kind, margin, state, source, target, sound, band):
    scale = courant / 12.0
    row, end = PAD - margin, PAD + TILE + margin
    while row < end:
        rows = 16 if end - row > 8 else 8
        here = pl.ds(row, rows)
        for w in range(2):
            centre = [source[w, f, here, :] for f in range(4)]
            dx = [slope_rows(source, w, f, row, rows) for f in range(4)]
            pair = jnp.concatenate(split(jnp.concatenate(centre[2:], axis=0)), axis=1)
            pair = jnp.dot(pair, band, preferred_element_type=jnp.float32)
            dy = [slope_lanes(centre[0]), slope_lanes(centre[1]), pair[:rows], pair[rows:]]
            diverge = dx[1] + dy[2]
            advect = [stream_speed * dx[f] + span_speed * dy[f] for f in range(4)]
            rate = [
                advect[0] + diverge,
                advect[1] + dx[3],
                advect[2] + dy[3],
                advect[3] + sound[w, 4, here, :] * diverge,
            ]
            for f in range(4):
                if kind == 1:
                    moved = centre[f] - scale * rate[f]
                elif kind == 2:
                    moved = 0.75 * state[w, f, here, :] + (0.25 * centre[f] - (0.25 * scale) * rate[f])
                else:
                    moved = (1.0 / 3.0) * state[w, f, here, :] + (
                        (2.0 / 3.0) * centre[f] - (2.0 / 3.0 * scale) * rate[f]
                    )
                target[w, f, here, :] = moved
        row += rows


def joined(wide, field, row, rows):
    here = pl.ds(PAD + row, rows)
    lane = lanes((rows, TILE))
    first = (lane >= HALO) & (lane < 64)
    both = jnp.where(first, wide[0, field, here, :], wide[1, field, here, :])
    return pltpu.roll(both, TILE - HALO, 1)


def spread(row):
    return jnp.broadcast_to(row, (8, TILE))


def inverse_factor(gram):
    count = MODES // 8
    lane, sub = lanes((8, TILE)), lax.broadcasted_iota(jnp.int32, (8, TILE), 0)
    tiles = [
        jnp.where(lane < MODES, gram[8 * r : 8 * r + 8], jnp.where(lane == MODES + 8 * r + sub, 1.0, 0.0))
        for r in range(count)
    ]
    for t in range(count):
        column = {
            (j, r): jnp.broadcast_to(tiles[r][:, 8 * t + j : 8 * t + j + 1], (8, TILE))
            for j in range(8)
            for r in range(t, count)
        }
        for j in range(0, 8, 2):
            corner, side = spread(column[j, t][j : j + 1, :]), spread(column[j + 1, t][j : j + 1, :])
            below, other = spread(column[j, t][j + 1 : j + 2, :]), spread(column[j + 1, t][j + 1 : j + 2, :])
            inverse_first = 1.0 / corner
            inverse_second = corner * (1.0 / (corner * other - below * side))
            ratio = below * inverse_first
            first = {r: column[j, r] * inverse_first for r in range(t, count)}
            first[t] = jnp.where(sub > j, first[t], 0.0)
            second = {r: (column[j + 1, r] - first[r] * side) * inverse_second for r in range(t, count)}
            second[t] = jnp.where(sub > j + 1, second[t], 0.0)
            for later in range(j + 2, 8):
                upper = spread(column[later, t][j : j + 1, :])
                lower = spread(column[later, t][j + 1 : j + 2, :]) - ratio * upper
                for r in range(t, count):
                    column[later, r] = column[later, r] - first[r] * upper - second[r] * lower
            upper = spread(tiles[t][j : j + 1, :])
            lower = spread(tiles[t][j + 1 : j + 2, :]) - ratio * upper
            for r in range(t, count):
                tiles[r] = tiles[r] - first[r] * upper - second[r] * lower
    rows = []
    for r in range(count):
        diagonal = jnp.sum(jnp.where(lane == 8 * r + sub, tiles[r], 0.0), axis=1, keepdims=True)
        scaled = pltpu.roll(tiles[r] * (1.0 / jnp.sqrt(diagonal)), MODES, 1)
        rows.append(jnp.where(lane < MODES, scaled, 0.0))
    return jnp.concatenate(rows, axis=0)


def fold(gram):
    half = MODES // 2
    wide = jnp.concatenate([gram, jnp.zeros_like(gram)], axis=1)
    early, late = wide[:half], wide[half:]
    row, lane = lax.broadcasted_iota(jnp.int32, (half, TILE), 0), lanes((half, TILE))
    diagonal = jnp.sum(jnp.where(lane == row + half, late, 0.0), axis=0, keepdims=True)
    mixed = jnp.where((lane >= half) & (lane <= row + half), pltpu.roll(early, half, 1), late)
    mixed = jnp.where((row == RESIDENT - half) & (lane < half), pltpu.roll(diagonal, TILE - half, 1), mixed)
    return mixed[: half // 2] + pltpu.roll(mixed[half // 2 :], MODES, 1)


def unfold(folded):
    half = MODES // 2
    row, lane = lax.broadcasted_iota(jnp.int32, (half, TILE), 0), lanes((half, TILE))
    mixed = jnp.concatenate([folded, pltpu.roll(folded, MODES, 1)], axis=0)
    diagonal = pltpu.roll(mixed[RESIDENT - half : RESIDENT - half + 1], half, 1)
    empty = (lane >= MODES) | ((lane < half) & (row >= RESIDENT - half))
    mixed = jnp.where(empty, 0.0, mixed)
    early = jnp.where(lane <= row, pltpu.roll(mixed, TILE - half, 1), 0.0)
    late = jnp.where((lane < half) | (lane > row + half), mixed, 0.0)
    whole = jnp.concatenate([early, late], axis=0)
    turned = jnp.concatenate([whole[:, :MODES].T, jnp.zeros((MODES, MODES), jnp.float32)], axis=1)
    row, lane = lax.broadcasted_iota(jnp.int32, (MODES, TILE), 0), lanes((MODES, TILE))
    middle = jnp.where(row < half, whole, jnp.where(row < RESIDENT, diagonal, 1.0))
    return jnp.where(row == lane, middle, whole + turned)


def exact_dot(a, b, contract):
    return lax.dot_general(
        a, b, (contract, ((), ())), precision=lax.Precision.HIGHEST, preferred_element_type=jnp.float32
    )


def turn(snap, block, group, first=0, last=TILE):
    modes = pl.ds(group * 16, 16)
    for row in range(first, last, 16):
        turned = jnp.swapaxes(snap[modes, row : row + 16, :], 0, 1)
        for i in range(16):
            block[modes, (row + i) * TILE : (row + i + 1) * TILE] = turned[i]


def wide_kernel(
    flow_hbm, sound_hbm, snap_hbm, state_out, block, inverse_out, normal_out, late_out,
    snap, tile, wide, one, two, strip, left_strip, right_strip,
    packed, part_one, part_two, total_two,
    line, late, late_one, late_two, late_total,
    reach_sem, load_sem, halo_send, halo_recv, sum_send, sum_recv,
):
    gx, gy = lax.axis_index("gx"), lax.axis_index("gy")
    core = lax.rem(gy, 2)
    cells = GX * GY * TILE * TILE

    def at(dx, dy):
        return (lax.rem(gx + (dx + GX), GX), lax.rem(gy + (dy + GY), GY))

    x, z, y = gx // 8, lax.rem(gx, 8), gy // 2
    row_steps = sorted(
        ((dx, dz) for dx in range(4) for dz in range(8) if dx or dz),
        key=lambda step: -min(step[0], 4 - step[0]) - min(step[1], 8 - step[1]),
    )
    row_peers = [(lax.rem(x + dx, 4) * 8 + lax.rem(z + dz, 8), gy) for dx, dz in row_steps]
    column_steps = sorted(
        ((dy, dc) for dy in range(4) for dc in range(2) if dy or dc), key=lambda step: -min(step[0], 4 - step[0])
    )
    column_peers = [(gx, lax.rem(y + dy, 4) * 2 + lax.rem(core + dc, 2)) for dy, dc in column_steps]
    corner_peers = [at(dx, dy) for dx in (-1, 1) for dy in (-1, 1)]
    near_peers = [
        peer
        for (dx, dz), peer in zip(row_steps, row_peers)
        if min(dx, 4 - dx) + min(dz, 8 - dz) <= 2
    ]
    entered = near_peers + column_peers + corner_peers

    barrier = pltpu.get_barrier_semaphore()
    for peer in entered:
        pl.semaphore_signal(barrier, inc=1, device_id=peer, device_id_type=MESH)

    inside = pl.ds(PAD, TILE)
    loads = [
        pltpu.make_async_copy(flow_hbm, tile.at[pl.ds(0, 4), inside, :], load_sem.at[0]),
        pltpu.make_async_copy(sound_hbm, tile.at[4, inside, :], load_sem.at[1]),
    ] + [
        pltpu.make_async_copy(
            snap_hbm.at[:, pl.ds(part * 32, 32), :],
            snap.at[pl.ds(0, RESIDENT), pl.ds(part * 32, 32), :],
            load_sem.at[2 + part],
        )
        for part in range(4)
    ]
    for load in loads:
        load.start()
    line[...] = jnp.zeros((TILE, 8, TILE), jnp.float32)
    snap[RESIDENT:MODES] = jnp.zeros((MODES - RESIDENT, TILE, TILE), jnp.bfloat16)
    loads[0].wait()
    loads[1].wait()

    lane = lanes((16, TILE))
    for row in range(0, TILE, 16):
        gathered = pltpu.roll(tile[0, pl.ds(PAD + row, 16), :], HALO, 1)
        for f in range(1, FIELDS):
            moved = pltpu.roll(tile[f, pl.ds(PAD + row, 16), :], HALO + 24 * f, 1)
            gathered = jnp.where(lane >= 24 * f, moved, gathered)
        strip[pl.ds(row, 16), :] = gathered

    def products(first, last, so_far):
        for row in range(first, last, 16):
            if row % 32 == 0:
                loads[2 + row // 32].wait()
            for group in range(4):
                turn(snap, block, group, row, row + 16)
            piece = block[:, row * TILE : (row + 16) * TILE]
            so_far = so_far + lax.dot_general(
                piece, piece, (((1,), (1,)), ((), ())), preferred_element_type=jnp.float32
            )
        return so_far

    gram = products(0, EARLY_ROWS, jnp.zeros((MODES, MODES), jnp.float32))
    pl.semaphore_wait(barrier, len(entered))

    top, bottom = pl.ds(0, PAD), pl.ds(PAD + TILE, PAD)
    low, high = pl.ds(0, PAD), pl.ds(TILE - PAD, PAD)
    moves = [
        (tile.at[:, pl.ds(TILE, PAD), :], tile.at[:, top, :], at(1, 0)),
        (tile.at[:, pl.ds(PAD, PAD), :], tile.at[:, bottom, :], at(-1, 0)),
        (strip, left_strip.at[inside, :], at(0, 1)),
        (strip, right_strip.at[inside, :], at(0, -1)),
        (strip.at[high, :], left_strip.at[top, :], at(1, 1)),
        (strip.at[low, :], left_strip.at[bottom, :], at(-1, 1)),
        (strip.at[high, :], right_strip.at[top, :], at(1, -1)),
        (strip.at[low, :], right_strip.at[bottom, :], at(-1, -1)),
    ]
    halos = []
    for number, (source, target, peer) in enumerate(moves):
        halos.append(
            pltpu.make_async_remote_copy(
                src_ref=source, dst_ref=target, send_sem=halo_send.at[number],
                recv_sem=halo_recv.at[number], device_id=peer, device_id_type=MESH,
            )
        )
        halos[-1].start()

    def send(source, target, slot, peer):
        copy = pltpu.make_async_remote_copy(
            src_ref=source, dst_ref=target, send_sem=sum_send.at[slot],
            recv_sem=sum_recv.at[slot], device_id=peer, device_id_type=MESH,
        )
        copy.start()
        return copy

    def received(ref, slot):
        pltpu.make_async_copy(ref, ref, sum_recv.at[slot]).wait()

    def sent(ref, slot):
        pltpu.make_async_copy(ref, ref, sum_send.at[slot]).wait()

    def pass_on(step):
        for peer in near_peers:
            pl.semaphore_signal(reach_sem.at[step], inc=1, device_id=peer, device_id_type=MESH)

    pass_on(0)

    gram = products(EARLY_ROWS, TILE, gram) * (1.0 / cells)
    packed[...] = fold(gram)

    for number, peer in enumerate(column_peers):
        send(packed, part_one.at[number], 0, peer)

    pl.semaphore_wait(reach_sem.at[0], len(near_peers))
    pass_on(1)
    for halo in halos:
        halo.wait()
    for row in range(0, ROWS, 16):
        here = pl.ds(row, 16)
        merged = jnp.where(lax.rem(lane, 24) >= HALO, right_strip[here, :], left_strip[here, :])
        for f in range(FIELDS):
            beside = pltpu.roll(merged, TILE - 24 * f, 1) if f else merged
            turned = pltpu.roll(tile[f, here, :], HALO, 1)
            wide[0, f, here, :] = jnp.where(lane < HALO, beside, turned)
            wide[1, f, here, :] = jnp.where((lane >= HALO) & (lane < 2 * HALO), beside, turned)

    band = lane_band()
    stage(1, 10, wide, wide, one, wide, band)

    received(part_one, 0)
    total = packed[...]
    for number in range(GY - 1):
        total = total + part_one[number]
    total_two[...] = total
    pl.semaphore_wait(reach_sem.at[1], len(near_peers))
    for number, peer in enumerate(row_peers):
        send(total_two, part_two.at[number], 1, peer)

    stage(2, 8, wide, one, two, wide, band)
    stage(3, 6, wide, two, wide, wide, band)
    pressures = [joined(wide, 3, 0, TILE).astype(jnp.bfloat16)]
    snap[RESIDENT] = pressures[0]
    pressures[0] = pressures[0].astype(jnp.float32)
    line[:, 0, :] = pressures[0]
    stage(1, 4, wide, wide, one, wide, band)
    stage(2, 2, wide, one, two, wide, band)
    stage(3, 0, wide, two, wide, wide, band)
    pressures.append(joined(wide, 3, 0, TILE).astype(jnp.bfloat16))
    snap[RESIDENT + 1] = pressures[1]
    pressures[1] = pressures[1].astype(jnp.float32)
    line[:, 1, :] = pressures[1]

    flat = jnp.concatenate([line[i].astype(jnp.bfloat16) for i in range(TILE)], axis=1)
    fresh = lax.dot_general(flat, block[...], (((1,), (1,)), ((), ())), preferred_element_type=jnp.float32)

    def product(a, b):
        return jnp.sum(jnp.sum(pressures[a] * pressures[b], axis=0, keepdims=True), axis=1, keepdims=True)

    pair = jnp.concatenate([fresh[0:1], fresh[1:2]], axis=1)
    place = lanes((1, TILE))
    for where, value in ((62, product(0, 0)), (126, product(0, 1)), (127, product(1, 1))):
        pair = jnp.where(place == where, value, pair)
    late[...] = pair * (1.0 / cells)
    for number, peer in enumerate(column_peers):
        send(late, late_one.at[number], 3, peer)

    turn(snap, block, 3)

    for f in range(4):
        state_out[f] = joined(wide, f, 0, TILE)

    received(late_one, 3)
    late_total[...] = late[...] + jnp.sum(late_one[...], axis=0)
    for number, peer in enumerate(row_peers):
        send(late_total, late_two.at[number], 4, peer)

    received(part_two, 1)
    total = total_two[...]
    for number in range(GX - 1):
        total = total + part_two[number]

    early = inverse_factor(unfold(total))
    inverse_out[...] = early
    normal_out[...] = exact_dot(early, early, ((0,), (0,)))

    received(late_two, 4)
    late_out[...] = late_total[...] + jnp.sum(late_two[...], axis=0)

    sent(part_one, 0)
    sent(part_two, 1)
    sent(late_one, 3)
    sent(late_two, 4)


def last_rows(early, normal, pair):
    lane = lanes((1, TILE))
    first = jnp.where(lane < MODES, pair, 0.0)
    second = jnp.where(lane < MODES, pltpu.roll(pair, MODES, 1), 0.0)

    def pick(vector, place):
        return jnp.sum(jnp.where(lane == place, vector, 0.0), axis=1, keepdims=True)

    norm_first, norm_second, cross = pick(first, 62), pick(second, 63), pick(second, 62)
    known = lane < RESIDENT
    both = jnp.concatenate(
        [jnp.where(known, first, 0.0), jnp.where(known, second, 0.0), jnp.zeros((6, TILE), jnp.float32)], axis=0
    )
    along = exact_dot(both, early, ((1,), (1,)))
    back = exact_dot(both, normal, ((1,), (0,)))
    along_first, along_second = along[0:1], along[1:2]
    scale_first = 1.0 / jnp.sqrt(norm_first - jnp.sum(along_first * along_first, axis=1, keepdims=True))
    row_first = (jnp.where(lane == 62, 1.0, 0.0) - back[0:1]) * scale_first
    shared = (cross - jnp.sum(along_first * along_second, axis=1, keepdims=True)) * scale_first
    left = norm_second - jnp.sum(along_second * along_second, axis=1, keepdims=True) - shared * shared
    row_second = (jnp.where(lane == 63, 1.0, 0.0) - back[1:2] - shared * row_first) * (1.0 / jnp.sqrt(left))
    return row_first, row_second


AHEAD = 3
KNOWN = 48


def basis_kernel(
    early_ref, normal_ref, late_ref, block_ref, state_hbm, basis_hbm, state_out, basis, sem, ahead_sem, state_sem
):
    def weights(rows):
        return jnp.concatenate(split(rows[:, :MODES]), axis=1)

    def slab(number, weight, first, signal):
        part = block_ref[:, number * 8 * TILE : (number + 1) * 8 * TILE]
        rows = jnp.dot(weight, jnp.concatenate([part, part, part], axis=0), preferred_element_type=jnp.float32)
        stacked = jnp.stack([rows[:, i * TILE : (i + 1) * TILE] for i in range(8)], axis=0)
        modes, here = pl.ds(first, weight.shape[0]), pl.ds(number * 8, 8)
        basis[modes, here, :] = jnp.swapaxes(stacked, 0, 1)
        copy = pltpu.make_async_copy(basis.at[modes, here, :], basis_hbm.at[modes, here, :], signal)
        copy.start()
        return copy

    early = early_ref[...]
    known = weights(early[:KNOWN])
    copies = [slab(number, known, 0, ahead_sem.at[number]) for number in range(AHEAD)]
    row_first, row_second = last_rows(early, normal_ref[...], late_ref[...])
    rest = weights(jnp.concatenate([early[KNOWN:RESIDENT], row_first, row_second], axis=0))
    copies += [slab(number, rest, KNOWN, sem.at[number]) for number in range(AHEAD)]
    every = jnp.concatenate([known, rest], axis=0)
    copies += [slab(number, every, 0, sem.at[number]) for number in range(AHEAD, TILE // 8)]
    copies.append(pltpu.make_async_copy(state_hbm, state_out, state_sem))
    copies[-1].start()
    for copy in copies:
        copy.wait()


def first(flow_state, sound_speed_sq, snapshots):
    hbm = pl.BlockSpec(memory_space=pltpu.HBM)
    local = pl.BlockSpec(memory_space=pltpu.VMEM)
    f32, bf16 = jnp.float32, jnp.bfloat16
    wide = pltpu.VMEM((2, 4, ROWS, TILE), f32)
    return pl.pallas_call(
        wide_kernel,
        out_shape=(
            jax.ShapeDtypeStruct((4, TILE, TILE), f32),
            jax.ShapeDtypeStruct((MODES, TILE * TILE), bf16),
            jax.ShapeDtypeStruct((MODES, TILE), f32),
            jax.ShapeDtypeStruct((TILE, TILE), f32),
            jax.ShapeDtypeStruct((1, TILE), f32),
        ),
        in_specs=[hbm] * 3,
        out_specs=(local,) * 5,
        scratch_shapes=[
            pltpu.VMEM((MODES, TILE, TILE), bf16),
            pltpu.VMEM((FIELDS, ROWS, TILE), f32),
            pltpu.VMEM((2, FIELDS, ROWS, TILE), f32),
            wide,
            wide,
            pltpu.VMEM((TILE, TILE), f32),
            pltpu.VMEM((ROWS, TILE), f32),
            pltpu.VMEM((ROWS, TILE), f32),
            pltpu.VMEM((16, TILE), f32),
            pltpu.VMEM((GY - 1, 16, TILE), f32),
            pltpu.VMEM((GX - 1, 16, TILE), f32),
            pltpu.VMEM((16, TILE), f32),
            pltpu.VMEM((TILE, 8, TILE), f32),
            pltpu.VMEM((1, TILE), f32),
            pltpu.VMEM((GY - 1, 1, TILE), f32),
            pltpu.VMEM((GX - 1, 1, TILE), f32),
            pltpu.VMEM((1, TILE), f32),
            pltpu.SemaphoreType.REGULAR((2,)),
            pltpu.SemaphoreType.DMA((6,)),
            pltpu.SemaphoreType.DMA((8,)),
            pltpu.SemaphoreType.DMA((8,)),
            pltpu.SemaphoreType.DMA((5,)),
            pltpu.SemaphoreType.DMA((5,)),
        ],
        compiler_params=pltpu.CompilerParams(
            collective_id=0, has_side_effects=True, vmem_limit_bytes=40 << 20
        ),
        name="flow_and_gram",
    )(*(pltpu.with_memory_space_constraint(x, pltpu.HBM) for x in (flow_state, sound_speed_sq, snapshots)))


def body(flow_state, sound_speed_sq, snapshots):
    new_state, block, early, normal, late = first(flow_state, sound_speed_sq, snapshots)
    local = pl.BlockSpec(memory_space=pltpu.VMEM)
    anywhere = pl.BlockSpec(memory_space=pl.ANY)
    hbm = pl.BlockSpec(memory_space=pltpu.HBM)
    f32 = jnp.float32
    pod_basis, new_state = pl.pallas_call(
        basis_kernel,
        out_shape=(
            jax.ShapeDtypeStruct((MODES, TILE, TILE), f32),
            jax.ShapeDtypeStruct((4, TILE, TILE), f32),
        ),
        in_specs=[local] * 4 + [anywhere],
        out_specs=(hbm, hbm),
        scratch_shapes=[
            pltpu.VMEM((MODES, TILE, TILE), f32),
            pltpu.SemaphoreType.DMA((TILE // 8,)),
            pltpu.SemaphoreType.DMA((AHEAD,)),
            pltpu.SemaphoreType.DMA,
        ],
        compiler_params=pltpu.CompilerParams(vmem_limit_bytes=20 << 20),
        name="basis",
    )(early, normal, late, block, new_state)
    return new_state, pod_basis


def solution(mesh):
    placed = (P(None, "gx", "gy"), P("gx", "gy"), P(None, "gx", "gy"))
    return jax.shard_map(
        body,
        mesh=mesh,
        in_specs=placed,
        out_specs=(P(None, "gx", "gy"), P(None, "gx", "gy")),
        check_vma=False,
    )
```

```python
import jax
import jax.numpy as jnp
from jax import lax
from jax.experimental import pallas as pl
from jax.experimental.pallas import tpu as pltpu
from jax.sharding import PartitionSpec as P

MESH = pl.DeviceIdType.MESH
STEPS = 2
courant = 0.8
stream_speed = 0.3
span_speed = 0.1

MODES = 64
RESIDENT = 62
TILE = 128
EARLY_ROWS = 64
HALO = 12
PAD = 16
ROWS = TILE + 2 * PAD
FIELDS = 5
GX = 32
GY = 8


def lanes(shape):
    return lax.broadcasted_iota(jnp.int32, shape, len(shape) - 1)


def slope_rows(ref, window, field, row, rows):
    near = ref[window, field, pl.ds(row + 1, rows), :] - ref[window, field, pl.ds(row - 1, rows), :]
    far = ref[window, field, pl.ds(row + 2, rows), :] - ref[window, field, pl.ds(row - 2, rows), :]
    return 8.0 * near - far


def slope_lanes(value):
    near = pltpu.roll(value, TILE - 1, 1) - pltpu.roll(value, 1, 1)
    far = pltpu.roll(value, TILE - 2, 1) - pltpu.roll(value, 2, 1)
    return 8.0 * near - far


def lane_band():
    away = lax.rem(
        lax.broadcasted_iota(jnp.int32, (TILE, TILE), 0) - lanes((TILE, TILE)) + TILE, TILE
    )
    band = jnp.where(away == 1, 8.0, jnp.where(away == TILE - 1, -8.0, 0.0))
    band = jnp.where(away == 2, -1.0, jnp.where(away == TILE - 2, 1.0, band)).astype(jnp.bfloat16)
    return jnp.concatenate([band, band, band], axis=0)


def split(value):
    high = value.astype(jnp.bfloat16)
    rest = value - high.astype(jnp.float32)
    middle = rest.astype(jnp.bfloat16)
    return [high, middle, (rest - middle.astype(jnp.float32)).astype(jnp.bfloat16)]


def stage(kind, margin, state, source, target, sound, band):
    scale = courant / 12.0
    row, end = PAD - margin, PAD + TILE + margin
    while row < end:
        rows = 16 if end - row > 8 else 8
        here = pl.ds(row, rows)
        for w in range(2):
            centre = [source[w, f, here, :] for f in range(4)]
            dx = [slope_rows(source, w, f, row, rows) for f in range(4)]
            pair = jnp.concatenate(split(jnp.concatenate(centre[2:], axis=0)), axis=1)
            pair = jnp.dot(pair, band, preferred_element_type=jnp.float32)
            dy = [slope_lanes(centre[0]), slope_lanes(centre[1]), pair[:rows], pair[rows:]]
            diverge = dx[1] + dy[2]
            advect = [stream_speed * dx[f] + span_speed * dy[f] for f in range(4)]
            rate = [
                advect[0] + diverge,
                advect[1] + dx[3],
                advect[2] + dy[3],
                advect[3] + sound[w, 4, here, :] * diverge,
            ]
            for f in range(4):
                if kind == 1:
                    moved = centre[f] - scale * rate[f]
                elif kind == 2:
                    moved = 0.75 * state[w, f, here, :] + (0.25 * centre[f] - (0.25 * scale) * rate[f])
                else:
                    moved = (1.0 / 3.0) * state[w, f, here, :] + (
                        (2.0 / 3.0) * centre[f] - (2.0 / 3.0 * scale) * rate[f]
                    )
                target[w, f, here, :] = moved
        row += rows


def joined(wide, field, row, rows):
    here = pl.ds(PAD + row, rows)
    lane = lanes((rows, TILE))
    first = (lane >= HALO) & (lane < 64)
    both = jnp.where(first, wide[0, field, here, :], wide[1, field, here, :])
    return pltpu.roll(both, TILE - HALO, 1)


def spread(row):
    return jnp.broadcast_to(row, (8, TILE))


def inverse_factor(gram):
    count = MODES // 8
    lane, sub = lanes((8, TILE)), lax.broadcasted_iota(jnp.int32, (8, TILE), 0)
    tiles = [
        jnp.where(lane < MODES, gram[8 * r : 8 * r + 8], jnp.where(lane == MODES + 8 * r + sub, 1.0, 0.0))
        for r in range(count)
    ]
    for t in range(count):
        column = {
            (j, r): jnp.broadcast_to(tiles[r][:, 8 * t + j : 8 * t + j + 1], (8, TILE))
            for j in range(8)
            for r in range(t, count)
        }
        for j in range(0, 8, 2):
            corner, side = spread(column[j, t][j : j + 1, :]), spread(column[j + 1, t][j : j + 1, :])
            below, other = spread(column[j, t][j + 1 : j + 2, :]), spread(column[j + 1, t][j + 1 : j + 2, :])
            inverse_first = 1.0 / corner
            inverse_second = corner * (1.0 / (corner * other - below * side))
            ratio = below * inverse_first
            first = {r: column[j, r] * inverse_first for r in range(t, count)}
            first[t] = jnp.where(sub > j, first[t], 0.0)
            second = {r: (column[j + 1, r] - first[r] * side) * inverse_second for r in range(t, count)}
            second[t] = jnp.where(sub > j + 1, second[t], 0.0)
            for later in range(j + 2, 8):
                upper = spread(column[later, t][j : j + 1, :])
                lower = spread(column[later, t][j + 1 : j + 2, :]) - ratio * upper
                for r in range(t, count):
                    column[later, r] = column[later, r] - first[r] * upper - second[r] * lower
            upper = spread(tiles[t][j : j + 1, :])
            lower = spread(tiles[t][j + 1 : j + 2, :]) - ratio * upper
            for r in range(t, count):
                tiles[r] = tiles[r] - first[r] * upper - second[r] * lower
    rows = []
    for r in range(count):
        diagonal = jnp.sum(jnp.where(lane == 8 * r + sub, tiles[r], 0.0), axis=1, keepdims=True)
        scaled = pltpu.roll(tiles[r] * (1.0 / jnp.sqrt(diagonal)), MODES, 1)
        rows.append(jnp.where(lane < MODES, scaled, 0.0))
    return jnp.concatenate(rows, axis=0)


def fold(gram):
    half = MODES // 2
    wide = jnp.concatenate([gram, jnp.zeros_like(gram)], axis=1)
    early, late = wide[:half], wide[half:]
    row, lane = lax.broadcasted_iota(jnp.int32, (half, TILE), 0), lanes((half, TILE))
    diagonal = jnp.sum(jnp.where(lane == row + half, late, 0.0), axis=0, keepdims=True)
    mixed = jnp.where((lane >= half) & (lane <= row + half), pltpu.roll(early, half, 1), late)
    mixed = jnp.where((row == RESIDENT - half) & (lane < half), pltpu.roll(diagonal, TILE - half, 1), mixed)
    return mixed[: half // 2] + pltpu.roll(mixed[half // 2 :], MODES, 1)


def unfold(folded):
    half = MODES // 2
    row, lane = lax.broadcasted_iota(jnp.int32, (half, TILE), 0), lanes((half, TILE))
    mixed = jnp.concatenate([folded, pltpu.roll(folded, MODES, 1)], axis=0)
    diagonal = pltpu.roll(mixed[RESIDENT - half : RESIDENT - half + 1], half, 1)
    empty = (lane >= MODES) | ((lane < half) & (row >= RESIDENT - half))
    mixed = jnp.where(empty, 0.0, mixed)
    early = jnp.where(lane <= row, pltpu.roll(mixed, TILE - half, 1), 0.0)
    late = jnp.where((lane < half) | (lane > row + half), mixed, 0.0)
    whole = jnp.concatenate([early, late], axis=0)
    turned = jnp.concatenate([whole[:, :MODES].T, jnp.zeros((MODES, MODES), jnp.float32)], axis=1)
    row, lane = lax.broadcasted_iota(jnp.int32, (MODES, TILE), 0), lanes((MODES, TILE))
    middle = jnp.where(row < half, whole, jnp.where(row < RESIDENT, diagonal, 1.0))
    return jnp.where(row == lane, middle, whole + turned)


def exact_dot(a, b, contract):
    return lax.dot_general(
        a, b, (contract, ((), ())), precision=lax.Precision.HIGHEST, preferred_element_type=jnp.float32
    )


def turn(snap, block, group, first=0, last=TILE):
    modes = pl.ds(group * 16, 16)
    for row in range(first, last, 16):
        turned = jnp.swapaxes(snap[modes, row : row + 16, :], 0, 1)
        for i in range(16):
            block[modes, (row + i) * TILE : (row + i + 1) * TILE] = turned[i]


def wide_kernel(
    flow_hbm, sound_hbm, snap_hbm, state_out, block, inverse_out, normal_out, late_out,
    snap, tile, wide, one, two, strip, left_strip, right_strip,
    packed, part_one, part_two, total_two,
    line, late, late_one, late_two, late_total,
    reach_sem, load_sem, halo_send, halo_recv, sum_send, sum_recv,
):
    gx, gy = lax.axis_index("gx"), lax.axis_index("gy")
    core = lax.rem(gy, 2)
    cells = GX * GY * TILE * TILE

    def at(dx, dy):
        return (lax.rem(gx + (dx + GX), GX), lax.rem(gy + (dy + GY), GY))

    x, z, y = gx // 8, lax.rem(gx, 8), gy // 2
    row_steps = sorted(
        ((dx, dz) for dx in range(4) for dz in range(8) if dx or dz),
        key=lambda step: -min(step[0], 4 - step[0]) - min(step[1], 8 - step[1]),
    )
    row_peers = [(lax.rem(x + dx, 4) * 8 + lax.rem(z + dz, 8), gy) for dx, dz in row_steps]
    column_steps = sorted(
        ((dy, dc) for dy in range(4) for dc in range(2) if dy or dc), key=lambda step: -min(step[0], 4 - step[0])
    )
    column_peers = [(gx, lax.rem(y + dy, 4) * 2 + lax.rem(core + dc, 2)) for dy, dc in column_steps]
    chip_steps = sorted(
        ((dx, dy, dz) for dx in range(4) for dy in range(4) for dz in range(8) if dx or dy or dz),
        key=lambda step: -min(step[0], 4 - step[0]) - min(step[1], 4 - step[1]) - min(step[2], 8 - step[2]),
    )
    chip_peers = [
        (lax.rem(x + dx, 4) * 8 + lax.rem(z + dz, 8), lax.rem(y + dy, 4) * 2 + core) for dx, dy, dz in chip_steps
    ]
    partner = (gx, gy + 1 - 2 * core)
    corner_peers = [at(dx, dy) for dx in (-1, 1) for dy in (-1, 1)]
    near_peers = [
        peer
        for (dx, dz), peer in zip(row_steps, row_peers)
        if min(dx, 4 - dx) + min(dz, 8 - dz) <= 2
    ]
    entered = near_peers + column_peers + corner_peers

    barrier = pltpu.get_barrier_semaphore()
    for peer in entered:
        pl.semaphore_signal(barrier, inc=1, device_id=peer, device_id_type=MESH)

    inside = pl.ds(PAD, TILE)
    loads = [
        pltpu.make_async_copy(flow_hbm, tile.at[pl.ds(0, 4), inside, :], load_sem.at[0]),
        pltpu.make_async_copy(sound_hbm, tile.at[4, inside, :], load_sem.at[1]),
    ] + [
        pltpu.make_async_copy(
            snap_hbm.at[:, pl.ds(part * 32, 32), :],
            snap.at[pl.ds(0, RESIDENT), pl.ds(part * 32, 32), :],
            load_sem.at[2 + part],
        )
        for part in range(4)
    ]
    for load in loads:
        load.start()
    line[...] = jnp.zeros((TILE, 8, TILE), jnp.float32)
    snap[RESIDENT:MODES] = jnp.zeros((MODES - RESIDENT, TILE, TILE), jnp.bfloat16)
    loads[0].wait()
    loads[1].wait()

    lane = lanes((16, TILE))
    for row in range(0, TILE, 16):
        gathered = pltpu.roll(tile[0, pl.ds(PAD + row, 16), :], HALO, 1)
        for f in range(1, FIELDS):
            moved = pltpu.roll(tile[f, pl.ds(PAD + row, 16), :], HALO + 24 * f, 1)
            gathered = jnp.where(lane >= 24 * f, moved, gathered)
        strip[pl.ds(row, 16), :] = gathered

    def products(first, last, so_far):
        for row in range(first, last, 16):
            if row % 32 == 0:
                loads[2 + row // 32].wait()
            for group in range(4):
                turn(snap, block, group, row, row + 16)
            piece = block[:, row * TILE : (row + 16) * TILE]
            so_far = so_far + lax.dot_general(
                piece, piece, (((1,), (1,)), ((), ())), preferred_element_type=jnp.float32
            )
        return so_far

    gram = products(0, EARLY_ROWS, jnp.zeros((MODES, MODES), jnp.float32))
    pl.semaphore_wait(barrier, len(entered))

    top, bottom = pl.ds(0, PAD), pl.ds(PAD + TILE, PAD)
    low, high = pl.ds(0, PAD), pl.ds(TILE - PAD, PAD)
    moves = [
        (tile.at[:, pl.ds(TILE, PAD), :], tile.at[:, top, :], at(1, 0)),
        (tile.at[:, pl.ds(PAD, PAD), :], tile.at[:, bottom, :], at(-1, 0)),
        (strip, left_strip.at[inside, :], at(0, 1)),
        (strip, right_strip.at[inside, :], at(0, -1)),
        (strip.at[high, :], left_strip.at[top, :], at(1, 1)),
        (strip.at[low, :], left_strip.at[bottom, :], at(-1, 1)),
        (strip.at[high, :], right_strip.at[top, :], at(1, -1)),
        (strip.at[low, :], right_strip.at[bottom, :], at(-1, -1)),
    ]
    halos = []
    for number, (source, target, peer) in enumerate(moves):
        halos.append(
            pltpu.make_async_remote_copy(
                src_ref=source, dst_ref=target, send_sem=halo_send.at[number],
                recv_sem=halo_recv.at[number], device_id=peer, device_id_type=MESH,
            )
        )
        halos[-1].start()

    def send(source, target, slot, peer):
        copy = pltpu.make_async_remote_copy(
            src_ref=source, dst_ref=target, send_sem=sum_send.at[slot],
            recv_sem=sum_recv.at[slot], device_id=peer, device_id_type=MESH,
        )
        copy.start()
        return copy

    def received(ref, slot):
        pltpu.make_async_copy(ref, ref, sum_recv.at[slot]).wait()

    def sent(ref, slot):
        pltpu.make_async_copy(ref, ref, sum_send.at[slot]).wait()

    def pass_on(step, peers):
        for peer in peers:
            pl.semaphore_signal(reach_sem.at[step], inc=1, device_id=peer, device_id_type=MESH)

    pass_on(0, near_peers)

    gram = products(EARLY_ROWS, TILE, gram) * (1.0 / cells)
    packed[...] = fold(gram)

    for number, peer in enumerate(column_peers):
        send(packed, part_one.at[number], 0, peer)

    pl.semaphore_wait(reach_sem.at[0], len(near_peers))
    pass_on(1, near_peers)
    for halo in halos:
        halo.wait()
    for row in range(0, ROWS, 16):
        here = pl.ds(row, 16)
        merged = jnp.where(lax.rem(lane, 24) >= HALO, right_strip[here, :], left_strip[here, :])
        for f in range(FIELDS):
            beside = pltpu.roll(merged, TILE - 24 * f, 1) if f else merged
            turned = pltpu.roll(tile[f, here, :], HALO, 1)
            wide[0, f, here, :] = jnp.where(lane < HALO, beside, turned)
            wide[1, f, here, :] = jnp.where((lane >= HALO) & (lane < 2 * HALO), beside, turned)

    band = lane_band()
    stage(1, 10, wide, wide, one, wide, band)

    received(part_one, 0)
    total = packed[...]
    for number in range(GY - 1):
        total = total + part_one[number]
    total_two[...] = total
    pl.semaphore_wait(reach_sem.at[1], len(near_peers))
    pass_on(2, column_peers)
    for number, peer in enumerate(row_peers):
        send(total_two, part_two.at[number], 1, peer)

    stage(2, 8, wide, one, two, wide, band)
    stage(3, 6, wide, two, wide, wide, band)
    pressures = [joined(wide, 3, 0, TILE).astype(jnp.bfloat16)]
    snap[RESIDENT] = pressures[0]
    pressures[0] = pressures[0].astype(jnp.float32)
    line[:, 0, :] = pressures[0]
    stage(1, 4, wide, wide, one, wide, band)
    stage(2, 2, wide, one, two, wide, band)
    stage(3, 0, wide, two, wide, wide, band)
    pressures.append(joined(wide, 3, 0, TILE).astype(jnp.bfloat16))
    snap[RESIDENT + 1] = pressures[1]
    pressures[1] = pressures[1].astype(jnp.float32)
    line[:, 1, :] = pressures[1]

    flat = jnp.concatenate([line[i].astype(jnp.bfloat16) for i in range(TILE)], axis=1)
    fresh = lax.dot_general(flat, block[...], (((1,), (1,)), ((), ())), preferred_element_type=jnp.float32)

    def product(a, b):
        return jnp.sum(jnp.sum(pressures[a] * pressures[b], axis=0, keepdims=True), axis=1, keepdims=True)

    pair = jnp.concatenate([fresh[0:1], fresh[1:2]], axis=1)
    place = lanes((1, TILE))
    for where, value in ((62, product(0, 0)), (126, product(0, 1)), (127, product(1, 1))):
        pair = jnp.where(place == where, value, pair)
    late[...] = pair * (1.0 / cells)
    swap = send(late, late_one, 3, partner)

    pl.semaphore_wait(reach_sem.at[2], len(column_peers))
    swap.wait()
    late_total[...] = late[...] + late_one[...]
    for number, peer in enumerate(chip_peers):
        send(late_total, late_two.at[number], 4, peer)

    turn(snap, block, 3)
    for f in range(4):
        state_out[f] = joined(wide, f, 0, TILE)

    received(part_two, 1)
    total = total_two[...]
    for number in range(GX - 1):
        total = total + part_two[number]

    early = inverse_factor(unfold(total))
    inverse_out[...] = early
    normal_out[...] = exact_dot(early, early, ((0,), (0,)))

    received(late_two, 4)
    parts = [late_two[number] for number in range(8)]
    for number in range(8, len(chip_peers)):
        parts[number % 8] = parts[number % 8] + late_two[number]
    while len(parts) > 1:
        parts = [a + b for a, b in zip(parts[::2], parts[1::2])]
    late_out[...] = late_total[...] + parts[0]

    sent(part_one, 0)
    sent(part_two, 1)
    sent(late_two, 4)


def last_rows(early, normal, pair):
    lane = lanes((1, TILE))
    first = jnp.where(lane < MODES, pair, 0.0)
    second = jnp.where(lane < MODES, pltpu.roll(pair, MODES, 1), 0.0)

    def pick(vector, place):
        return jnp.sum(jnp.where(lane == place, vector, 0.0), axis=1, keepdims=True)

    norm_first, norm_second, cross = pick(first, 62), pick(second, 63), pick(second, 62)
    known = lane < RESIDENT
    both = jnp.concatenate(
        [jnp.where(known, first, 0.0), jnp.where(known, second, 0.0), jnp.zeros((6, TILE), jnp.float32)], axis=0
    )
    along = exact_dot(both, early, ((1,), (1,)))
    back = exact_dot(both, normal, ((1,), (0,)))
    along_first, along_second = along[0:1], along[1:2]
    scale_first = 1.0 / jnp.sqrt(norm_first - jnp.sum(along_first * along_first, axis=1, keepdims=True))
    row_first = (jnp.where(lane == 62, 1.0, 0.0) - back[0:1]) * scale_first
    shared = (cross - jnp.sum(along_first * along_second, axis=1, keepdims=True)) * scale_first
    left = norm_second - jnp.sum(along_second * along_second, axis=1, keepdims=True) - shared * shared
    row_second = (jnp.where(lane == 63, 1.0, 0.0) - back[1:2] - shared * row_first) * (1.0 / jnp.sqrt(left))
    return row_first, row_second


def basis_kernel(
    early_ref, normal_ref, late_ref, block_ref, state_hbm, basis_hbm, state_out, basis, sem, state_sem
):
    def weights(rows):
        return jnp.concatenate(split(rows[:, :MODES]), axis=1)

    def slab(number, weight):
        part = block_ref[:, number * 8 * TILE : (number + 1) * 8 * TILE]
        rows = jnp.dot(weight, jnp.concatenate([part, part, part], axis=0), preferred_element_type=jnp.float32)
        stacked = jnp.stack([rows[:, i * TILE : (i + 1) * TILE] for i in range(8)], axis=0)
        here = pl.ds(number * 8, 8)
        basis[:, here, :] = jnp.swapaxes(stacked, 0, 1)
        copy = pltpu.make_async_copy(basis.at[:, here, :], basis_hbm.at[:, here, :], sem.at[number])
        copy.start()
        return copy

    early = early_ref[...]
    row_first, row_second = last_rows(early, normal_ref[...], late_ref[...])
    weight = weights(jnp.concatenate([early[:RESIDENT], row_first, row_second], axis=0))
    copies = [slab(number, weight) for number in range(TILE // 8)]
    copies.append(pltpu.make_async_copy(state_hbm, state_out, state_sem))
    copies[-1].start()
    for copy in copies:
        copy.wait()


def first(flow_state, sound_speed_sq, snapshots):
    hbm = pl.BlockSpec(memory_space=pltpu.HBM)
    local = pl.BlockSpec(memory_space=pltpu.VMEM)
    f32, bf16 = jnp.float32, jnp.bfloat16
    wide = pltpu.VMEM((2, 4, ROWS, TILE), f32)
    return pl.pallas_call(
        wide_kernel,
        out_shape=(
            jax.ShapeDtypeStruct((4, TILE, TILE), f32),
            jax.ShapeDtypeStruct((MODES, TILE * TILE), bf16),
            jax.ShapeDtypeStruct((MODES, TILE), f32),
            jax.ShapeDtypeStruct((TILE, TILE), f32),
            jax.ShapeDtypeStruct((1, TILE), f32),
        ),
        in_specs=[hbm] * 3,
        out_specs=(local,) * 5,
        scratch_shapes=[
            pltpu.VMEM((MODES, TILE, TILE), bf16),
            pltpu.VMEM((FIELDS, ROWS, TILE), f32),
            pltpu.VMEM((2, FIELDS, ROWS, TILE), f32),
            wide,
            wide,
            pltpu.VMEM((TILE, TILE), f32),
            pltpu.VMEM((ROWS, TILE), f32),
            pltpu.VMEM((ROWS, TILE), f32),
            pltpu.VMEM((16, TILE), f32),
            pltpu.VMEM((GY - 1, 16, TILE), f32),
            pltpu.VMEM((GX - 1, 16, TILE), f32),
            pltpu.VMEM((16, TILE), f32),
            pltpu.VMEM((TILE, 8, TILE), f32),
            pltpu.VMEM((1, TILE), f32),
            pltpu.VMEM((1, TILE), f32),
            pltpu.VMEM((GX * GY // 2 - 1, 1, TILE), f32),
            pltpu.VMEM((1, TILE), f32),
            pltpu.SemaphoreType.REGULAR((3,)),
            pltpu.SemaphoreType.DMA((6,)),
            pltpu.SemaphoreType.DMA((8,)),
            pltpu.SemaphoreType.DMA((8,)),
            pltpu.SemaphoreType.DMA((5,)),
            pltpu.SemaphoreType.DMA((5,)),
        ],
        compiler_params=pltpu.CompilerParams(
            collective_id=0, has_side_effects=True, vmem_limit_bytes=40 << 20
        ),
        name="flow_and_gram",
    )(*(pltpu.with_memory_space_constraint(x, pltpu.HBM) for x in (flow_state, sound_speed_sq, snapshots)))


def body(flow_state, sound_speed_sq, snapshots):
    new_state, block, early, normal, late = first(flow_state, sound_speed_sq, snapshots)
    local = pl.BlockSpec(memory_space=pltpu.VMEM)
    anywhere = pl.BlockSpec(memory_space=pl.ANY)
    hbm = pl.BlockSpec(memory_space=pltpu.HBM)
    f32 = jnp.float32
    pod_basis, new_state = pl.pallas_call(
        basis_kernel,
        out_shape=(
            jax.ShapeDtypeStruct((MODES, TILE, TILE), f32),
            jax.ShapeDtypeStruct((4, TILE, TILE), f32),
        ),
        in_specs=[local] * 4 + [anywhere],
        out_specs=(hbm, hbm),
        scratch_shapes=[
            pltpu.VMEM((MODES, TILE, TILE), f32),
            pltpu.SemaphoreType.DMA((TILE // 8,)),
            pltpu.SemaphoreType.DMA,
        ],
        compiler_params=pltpu.CompilerParams(vmem_limit_bytes=20 << 20),
        name="basis",
    )(early, normal, late, block, new_state)
    return new_state, pod_basis


def solution(mesh):
    placed = (P(None, "gx", "gy"), P("gx", "gy"), P(None, "gx", "gy"))
    return jax.shard_map(
        body,
        mesh=mesh,
        in_specs=placed,
        out_specs=(P(None, "gx", "gy"), P(None, "gx", "gy")),
        check_vma=False,
    )
```

```python
import jax
import jax.numpy as jnp
from jax import lax
from jax.experimental import pallas as pl
from jax.experimental.pallas import tpu as pltpu
from jax.sharding import PartitionSpec as P

MESH = pl.DeviceIdType.MESH
STEPS = 2
courant = 0.8
stream_speed = 0.3
span_speed = 0.1

MODES = 64
RESIDENT = 62
TILE = 128
EARLY_ROWS = 96
HALO = 12
PAD = 16
ROWS = TILE + 2 * PAD
FIELDS = 5
GX = 32
GY = 8


def lanes(shape):
    return lax.broadcasted_iota(jnp.int32, shape, len(shape) - 1)


def slope_rows(ref, window, field, row, rows):
    near = ref[window, field, pl.ds(row + 1, rows), :] - ref[window, field, pl.ds(row - 1, rows), :]
    far = ref[window, field, pl.ds(row + 2, rows), :] - ref[window, field, pl.ds(row - 2, rows), :]
    return 8.0 * near - far


def slope_lanes(value):
    near = pltpu.roll(value, TILE - 1, 1) - pltpu.roll(value, 1, 1)
    far = pltpu.roll(value, TILE - 2, 1) - pltpu.roll(value, 2, 1)
    return 8.0 * near - far


def lane_band():
    away = lax.rem(
        lax.broadcasted_iota(jnp.int32, (TILE, TILE), 0) - lanes((TILE, TILE)) + TILE, TILE
    )
    band = jnp.where(away == 1, 8.0, jnp.where(away == TILE - 1, -8.0, 0.0))
    band = jnp.where(away == 2, -1.0, jnp.where(away == TILE - 2, 1.0, band)).astype(jnp.bfloat16)
    return jnp.concatenate([band, band, band], axis=0)


def split(value):
    high = value.astype(jnp.bfloat16)
    rest = value - high.astype(jnp.float32)
    middle = rest.astype(jnp.bfloat16)
    return [high, middle, (rest - middle.astype(jnp.float32)).astype(jnp.bfloat16)]


def stage(kind, margin, state, source, target, sound, band):
    scale = courant / 12.0
    row, end = PAD - margin, PAD + TILE + margin
    while row < end:
        rows = 16 if end - row > 8 else 8
        here = pl.ds(row, rows)
        for w in range(2):
            centre = [source[w, f, here, :] for f in range(4)]
            dx = [slope_rows(source, w, f, row, rows) for f in range(4)]
            pair = jnp.concatenate(split(jnp.concatenate(centre[2:], axis=0)), axis=1)
            pair = jnp.dot(pair, band, preferred_element_type=jnp.float32)
            dy = [slope_lanes(centre[0]), slope_lanes(centre[1]), pair[:rows], pair[rows:]]
            diverge = dx[1] + dy[2]
            advect = [stream_speed * dx[f] + span_speed * dy[f] for f in range(4)]
            rate = [
                advect[0] + diverge,
                advect[1] + dx[3],
                advect[2] + dy[3],
                advect[3] + sound[w, 4, here, :] * diverge,
            ]
            for f in range(4):
                if kind == 1:
                    moved = centre[f] - scale * rate[f]
                elif kind == 2:
                    moved = 0.75 * state[w, f, here, :] + (0.25 * centre[f] - (0.25 * scale) * rate[f])
                else:
                    moved = (1.0 / 3.0) * state[w, f, here, :] + (
                        (2.0 / 3.0) * centre[f] - (2.0 / 3.0 * scale) * rate[f]
                    )
                target[w, f, here, :] = moved
        row += rows


def joined(wide, field, row, rows):
    here = pl.ds(PAD + row, rows)
    lane = lanes((rows, TILE))
    first = (lane >= HALO) & (lane < 64)
    both = jnp.where(first, wide[0, field, here, :], wide[1, field, here, :])
    return pltpu.roll(both, TILE - HALO, 1)


def spread(row):
    return jnp.broadcast_to(row, (8, TILE))


def inverse_factor(gram):
    count = MODES // 8
    lane, sub = lanes((8, TILE)), lax.broadcasted_iota(jnp.int32, (8, TILE), 0)
    tiles = [
        jnp.where(lane < MODES, gram[8 * r : 8 * r + 8], jnp.where(lane == MODES + 8 * r + sub, 1.0, 0.0))
        for r in range(count)
    ]
    for t in range(count):
        column = {
            (j, r): jnp.broadcast_to(tiles[r][:, 8 * t + j : 8 * t + j + 1], (8, TILE))
            for j in range(8)
            for r in range(t, count)
        }
        for j in range(0, 8, 2):
            corner, side = spread(column[j, t][j : j + 1, :]), spread(column[j + 1, t][j : j + 1, :])
            below, other = spread(column[j, t][j + 1 : j + 2, :]), spread(column[j + 1, t][j + 1 : j + 2, :])
            inverse_first = 1.0 / corner
            inverse_second = corner * (1.0 / (corner * other - below * side))
            ratio = below * inverse_first
            first = {r: column[j, r] * inverse_first for r in range(t, count)}
            first[t] = jnp.where(sub > j, first[t], 0.0)
            second = {r: (column[j + 1, r] - first[r] * side) * inverse_second for r in range(t, count)}
            second[t] = jnp.where(sub > j + 1, second[t], 0.0)
            for later in range(j + 2, 8):
                upper = spread(column[later, t][j : j + 1, :])
                lower = spread(column[later, t][j + 1 : j + 2, :]) - ratio * upper
                for r in range(t, count):
                    column[later, r] = column[later, r] - first[r] * upper - second[r] * lower
            upper = spread(tiles[t][j : j + 1, :])
            lower = spread(tiles[t][j + 1 : j + 2, :]) - ratio * upper
            for r in range(t, count):
                tiles[r] = tiles[r] - first[r] * upper - second[r] * lower
    rows = []
    for r in range(count):
        diagonal = jnp.sum(jnp.where(lane == 8 * r + sub, tiles[r], 0.0), axis=1, keepdims=True)
        scaled = pltpu.roll(tiles[r] * (1.0 / jnp.sqrt(diagonal)), MODES, 1)
        rows.append(jnp.where(lane < MODES, scaled, 0.0))
    return jnp.concatenate(rows, axis=0)


def fold(gram):
    half = MODES // 2
    wide = jnp.concatenate([gram, jnp.zeros_like(gram)], axis=1)
    early, late = wide[:half], wide[half:]
    row, lane = lax.broadcasted_iota(jnp.int32, (half, TILE), 0), lanes((half, TILE))
    diagonal = jnp.sum(jnp.where(lane == row + half, late, 0.0), axis=0, keepdims=True)
    mixed = jnp.where((lane >= half) & (lane <= row + half), pltpu.roll(early, half, 1), late)
    mixed = jnp.where((row == RESIDENT - half) & (lane < half), pltpu.roll(diagonal, TILE - half, 1), mixed)
    return mixed[: half // 2] + pltpu.roll(mixed[half // 2 :], MODES, 1)


def unfold(folded):
    half = MODES // 2
    row, lane = lax.broadcasted_iota(jnp.int32, (half, TILE), 0), lanes((half, TILE))
    mixed = jnp.concatenate([folded, pltpu.roll(folded, MODES, 1)], axis=0)
    diagonal = pltpu.roll(mixed[RESIDENT - half : RESIDENT - half + 1], half, 1)
    empty = (lane >= MODES) | ((lane < half) & (row >= RESIDENT - half))
    mixed = jnp.where(empty, 0.0, mixed)
    early = jnp.where(lane <= row, pltpu.roll(mixed, TILE - half, 1), 0.0)
    late = jnp.where((lane < half) | (lane > row + half), mixed, 0.0)
    whole = jnp.concatenate([early, late], axis=0)
    turned = jnp.concatenate([whole[:, :MODES].T, jnp.zeros((MODES, MODES), jnp.float32)], axis=1)
    row, lane = lax.broadcasted_iota(jnp.int32, (MODES, TILE), 0), lanes((MODES, TILE))
    middle = jnp.where(row < half, whole, jnp.where(row < RESIDENT, diagonal, 1.0))
    return jnp.where(row == lane, middle, whole + turned)


def exact_dot(a, b, contract):
    return lax.dot_general(
        a, b, (contract, ((), ())), precision=lax.Precision.HIGHEST, preferred_element_type=jnp.float32
    )


def turn(snap, block, group, first=0, last=TILE):
    modes = pl.ds(group * 16, 16)
    for row in range(first, last, 16):
        turned = jnp.swapaxes(snap[modes, row : row + 16, :], 0, 1)
        for i in range(16):
            block[modes, (row + i) * TILE : (row + i + 1) * TILE] = turned[i]


def wide_kernel(
    flow_hbm, sound_hbm, snap_hbm, state_out, block, inverse_out, normal_out, late_out,
    snap, tile, wide, one, two, strip, left_strip, right_strip,
    packed, part_one, part_two, total_two,
    line, late, late_one, late_two, late_total,
    reach_sem, load_sem, halo_send, halo_recv, sum_send, sum_recv,
):
    gx, gy = lax.axis_index("gx"), lax.axis_index("gy")
    core = lax.rem(gy, 2)
    cells = GX * GY * TILE * TILE

    def at(dx, dy):
        return (lax.rem(gx + (dx + GX), GX), lax.rem(gy + (dy + GY), GY))

    x, z, y = gx // 8, lax.rem(gx, 8), gy // 2
    row_steps = sorted(
        ((dx, dz) for dx in range(4) for dz in range(8) if dx or dz),
        key=lambda step: -min(step[0], 4 - step[0]) - min(step[1], 8 - step[1]),
    )
    row_peers = [(lax.rem(x + dx, 4) * 8 + lax.rem(z + dz, 8), gy) for dx, dz in row_steps]
    column_steps = sorted(
        ((dy, dc) for dy in range(4) for dc in range(2) if dy or dc), key=lambda step: -min(step[0], 4 - step[0])
    )
    column_peers = [(gx, lax.rem(y + dy, 4) * 2 + lax.rem(core + dc, 2)) for dy, dc in column_steps]
    chip_steps = sorted(
        ((dx, dy, dz) for dx in range(4) for dy in range(4) for dz in range(8) if dx or dy or dz),
        key=lambda step: -min(step[0], 4 - step[0]) - min(step[1], 4 - step[1]) - min(step[2], 8 - step[2]),
    )
    chip_peers = [
        (lax.rem(x + dx, 4) * 8 + lax.rem(z + dz, 8), lax.rem(y + dy, 4) * 2 + core) for dx, dy, dz in chip_steps
    ]
    partner = (gx, gy + 1 - 2 * core)
    corner_peers = [at(dx, dy) for dx in (-1, 1) for dy in (-1, 1)]
    near_peers = [
        peer
        for (dx, dz), peer in zip(row_steps, row_peers)
        if min(dx, 4 - dx) + min(dz, 8 - dz) <= 2
    ]
    entered = near_peers + column_peers + corner_peers

    barrier = pltpu.get_barrier_semaphore()
    for peer in entered:
        pl.semaphore_signal(barrier, inc=1, device_id=peer, device_id_type=MESH)

    inside = pl.ds(PAD, TILE)
    loads = [
        pltpu.make_async_copy(flow_hbm, tile.at[pl.ds(0, 4), inside, :], load_sem.at[0]),
        pltpu.make_async_copy(sound_hbm, tile.at[4, inside, :], load_sem.at[1]),
    ] + [
        pltpu.make_async_copy(
            snap_hbm.at[:, pl.ds(part * 32, 32), :],
            snap.at[pl.ds(0, RESIDENT), pl.ds(part * 32, 32), :],
            load_sem.at[2 + part],
        )
        for part in range(4)
    ]
    for load in loads:
        load.start()
    line[...] = jnp.zeros((TILE, 8, TILE), jnp.float32)
    snap[RESIDENT:MODES] = jnp.zeros((MODES - RESIDENT, TILE, TILE), jnp.bfloat16)
    loads[0].wait()
    loads[1].wait()

    lane = lanes((16, TILE))
    for row in range(0, TILE, 16):
        gathered = pltpu.roll(tile[0, pl.ds(PAD + row, 16), :], HALO, 1)
        for f in range(1, FIELDS):
            moved = pltpu.roll(tile[f, pl.ds(PAD + row, 16), :], HALO + 24 * f, 1)
            gathered = jnp.where(lane >= 24 * f, moved, gathered)
        strip[pl.ds(row, 16), :] = gathered

    def products(first, last, so_far):
        for row in range(first, last, 16):
            if row % 32 == 0:
                loads[2 + row // 32].wait()
            for group in range(4):
                turn(snap, block, group, row, row + 16)
            piece = block[:, row * TILE : (row + 16) * TILE]
            so_far = so_far + lax.dot_general(
                piece, piece, (((1,), (1,)), ((), ())), preferred_element_type=jnp.float32
            )
        return so_far

    gram = products(0, EARLY_ROWS, jnp.zeros((MODES, MODES), jnp.float32))
    pl.semaphore_wait(barrier, len(entered))

    top, bottom = pl.ds(0, PAD), pl.ds(PAD + TILE, PAD)
    low, high = pl.ds(0, PAD), pl.ds(TILE - PAD, PAD)
    moves = [
        (tile.at[:, pl.ds(TILE, PAD), :], tile.at[:, top, :], at(1, 0)),
        (tile.at[:, pl.ds(PAD, PAD), :], tile.at[:, bottom, :], at(-1, 0)),
        (strip, left_strip.at[inside, :], at(0, 1)),
        (strip, right_strip.at[inside, :], at(0, -1)),
        (strip.at[high, :], left_strip.at[top, :], at(1, 1)),
        (strip.at[low, :], left_strip.at[bottom, :], at(-1, 1)),
        (strip.at[high, :], right_strip.at[top, :], at(1, -1)),
        (strip.at[low, :], right_strip.at[bottom, :], at(-1, -1)),
    ]
    halos = []
    for number, (source, target, peer) in enumerate(moves):
        halos.append(
            pltpu.make_async_remote_copy(
                src_ref=source, dst_ref=target, send_sem=halo_send.at[number],
                recv_sem=halo_recv.at[number], device_id=peer, device_id_type=MESH,
            )
        )
        halos[-1].start()

    def send(source, target, slot, peer):
        copy = pltpu.make_async_remote_copy(
            src_ref=source, dst_ref=target, send_sem=sum_send.at[slot],
            recv_sem=sum_recv.at[slot], device_id=peer, device_id_type=MESH,
        )
        copy.start()
        return copy

    def received(ref, slot):
        pltpu.make_async_copy(ref, ref, sum_recv.at[slot]).wait()

    def sent(ref, slot):
        pltpu.make_async_copy(ref, ref, sum_send.at[slot]).wait()

    def pass_on(step, peers):
        for peer in peers:
            pl.semaphore_signal(reach_sem.at[step], inc=1, device_id=peer, device_id_type=MESH)

    pass_on(0, near_peers)

    gram = products(EARLY_ROWS, TILE, gram) * (1.0 / cells)
    packed[...] = fold(gram)

    for number, peer in enumerate(column_peers):
        send(packed, part_one.at[number], 0, peer)

    pl.semaphore_wait(reach_sem.at[0], len(near_peers))
    pass_on(1, near_peers)
    for row in range(PAD, PAD + TILE, 16):
        for f in range(FIELDS):
            wide[0, f, pl.ds(row, 16), :] = pltpu.roll(tile[f, pl.ds(row, 16), :], HALO, 1)
    for halo in halos:
        halo.wait()
    for row in range(0, ROWS, 16):
        here = pl.ds(row, 16)
        main = PAD <= row < PAD + TILE
        merged = jnp.where(lax.rem(lane, 24) >= HALO, right_strip[here, :], left_strip[here, :])
        for f in range(FIELDS):
            beside = pltpu.roll(merged, TILE - 24 * f, 1) if f else merged
            turned = wide[0, f, here, :] if main else pltpu.roll(tile[f, here, :], HALO, 1)
            wide[0, f, here, :] = jnp.where(lane < HALO, beside, turned)
            wide[1, f, here, :] = jnp.where((lane >= HALO) & (lane < 2 * HALO), beside, turned)

    band = lane_band()
    stage(1, 10, wide, wide, one, wide, band)

    received(part_one, 0)
    total = packed[...]
    for number in range(GY - 1):
        total = total + part_one[number]
    total_two[...] = total
    pl.semaphore_wait(reach_sem.at[1], len(near_peers))
    pass_on(2, column_peers)
    for number, peer in enumerate(row_peers):
        send(total_two, part_two.at[number], 1, peer)

    stage(2, 8, wide, one, two, wide, band)
    stage(3, 6, wide, two, wide, wide, band)
    pressures = [joined(wide, 3, 0, TILE).astype(jnp.bfloat16)]
    snap[RESIDENT] = pressures[0]
    pressures[0] = pressures[0].astype(jnp.float32)
    line[:, 0, :] = pressures[0]
    stage(1, 4, wide, wide, one, wide, band)
    stage(2, 2, wide, one, two, wide, band)
    stage(3, 0, wide, two, wide, wide, band)
    pressures.append(joined(wide, 3, 0, TILE).astype(jnp.bfloat16))
    snap[RESIDENT + 1] = pressures[1]
    pressures[1] = pressures[1].astype(jnp.float32)
    line[:, 1, :] = pressures[1]

    flat = jnp.concatenate([line[i].astype(jnp.bfloat16) for i in range(TILE)], axis=1)
    fresh = lax.dot_general(flat, block[...], (((1,), (1,)), ((), ())), preferred_element_type=jnp.float32)

    def product(a, b):
        return jnp.sum(jnp.sum(pressures[a] * pressures[b], axis=0, keepdims=True), axis=1, keepdims=True)

    pair = jnp.concatenate([fresh[0:1], fresh[1:2]], axis=1)
    place = lanes((1, TILE))
    for where, value in ((62, product(0, 0)), (126, product(0, 1)), (127, product(1, 1))):
        pair = jnp.where(place == where, value, pair)
    late[...] = pair * (1.0 / cells)
    swap = send(late, late_one, 3, partner)

    pl.semaphore_wait(reach_sem.at[2], len(column_peers))
    swap.wait()
    late_total[...] = late[...] + late_one[...]
    for number, peer in enumerate(chip_peers):
        send(late_total, late_two.at[number], 4, peer)

    turn(snap, block, 3)
    for f in range(4):
        state_out[f] = joined(wide, f, 0, TILE)

    received(part_two, 1)
    total = total_two[...]
    for number in range(GX - 1):
        total = total + part_two[number]

    early = inverse_factor(unfold(total))
    inverse_out[...] = early
    normal_out[...] = exact_dot(early, early, ((0,), (0,)))

    received(late_two, 4)
    parts = [late_two[number] for number in range(8)]
    for number in range(8, len(chip_peers)):
        parts[number % 8] = parts[number % 8] + late_two[number]
    while len(parts) > 1:
        parts = [a + b for a, b in zip(parts[::2], parts[1::2])]
    late_out[...] = late_total[...] + parts[0]

    sent(part_one, 0)
    sent(part_two, 1)
    sent(late_two, 4)


def last_rows(early, normal, pair):
    lane = lanes((1, TILE))
    first = jnp.where(lane < MODES, pair, 0.0)
    second = jnp.where(lane < MODES, pltpu.roll(pair, MODES, 1), 0.0)

    def pick(vector, place):
        return jnp.sum(jnp.where(lane == place, vector, 0.0), axis=1, keepdims=True)

    norm_first, norm_second, cross = pick(first, 62), pick(second, 63), pick(second, 62)
    known = lane < RESIDENT
    both = jnp.concatenate(
        [jnp.where(known, first, 0.0), jnp.where(known, second, 0.0), jnp.zeros((6, TILE), jnp.float32)], axis=0
    )
    along = exact_dot(both, early, ((1,), (1,)))
    back = exact_dot(both, normal, ((1,), (0,)))
    along_first, along_second = along[0:1], along[1:2]
    scale_first = 1.0 / jnp.sqrt(norm_first - jnp.sum(along_first * along_first, axis=1, keepdims=True))
    row_first = (jnp.where(lane == 62, 1.0, 0.0) - back[0:1]) * scale_first
    shared = (cross - jnp.sum(along_first * along_second, axis=1, keepdims=True)) * scale_first
    left = norm_second - jnp.sum(along_second * along_second, axis=1, keepdims=True) - shared * shared
    row_second = (jnp.where(lane == 63, 1.0, 0.0) - back[1:2] - shared * row_first) * (1.0 / jnp.sqrt(left))
    return row_first, row_second


def basis_kernel(
    early_ref, normal_ref, late_ref, block_ref, state_hbm, basis_hbm, state_out, basis, sem, state_sem
):
    def weights(rows):
        return jnp.concatenate(split(rows[:, :MODES]), axis=1)

    def slab(number, weight):
        part = block_ref[:, number * 8 * TILE : (number + 1) * 8 * TILE]
        rows = jnp.dot(weight, jnp.concatenate([part, part, part], axis=0), preferred_element_type=jnp.float32)
        stacked = jnp.stack([rows[:, i * TILE : (i + 1) * TILE] for i in range(8)], axis=0)
        here = pl.ds(number * 8, 8)
        basis[:, here, :] = jnp.swapaxes(stacked, 0, 1)
        copy = pltpu.make_async_copy(basis.at[:, here, :], basis_hbm.at[:, here, :], sem.at[number])
        copy.start()
        return copy

    early = early_ref[...]
    row_first, row_second = last_rows(early, normal_ref[...], late_ref[...])
    weight = weights(jnp.concatenate([early[:RESIDENT], row_first, row_second], axis=0))
    copies = [slab(number, weight) for number in range(TILE // 8)]
    copies.append(pltpu.make_async_copy(state_hbm, state_out, state_sem))
    copies[-1].start()
    for copy in copies:
        copy.wait()


def first(flow_state, sound_speed_sq, snapshots):
    hbm = pl.BlockSpec(memory_space=pltpu.HBM)
    local = pl.BlockSpec(memory_space=pltpu.VMEM)
    f32, bf16 = jnp.float32, jnp.bfloat16
    wide = pltpu.VMEM((2, 4, ROWS, TILE), f32)
    return pl.pallas_call(
        wide_kernel,
        out_shape=(
            jax.ShapeDtypeStruct((4, TILE, TILE), f32),
            jax.ShapeDtypeStruct((MODES, TILE * TILE), bf16),
            jax.ShapeDtypeStruct((MODES, TILE), f32),
            jax.ShapeDtypeStruct((TILE, TILE), f32),
            jax.ShapeDtypeStruct((1, TILE), f32),
        ),
        in_specs=[hbm] * 3,
        out_specs=(local,) * 5,
        scratch_shapes=[
            pltpu.VMEM((MODES, TILE, TILE), bf16),
            pltpu.VMEM((FIELDS, ROWS, TILE), f32),
            pltpu.VMEM((2, FIELDS, ROWS, TILE), f32),
            wide,
            wide,
            pltpu.VMEM((TILE, TILE), f32),
            pltpu.VMEM((ROWS, TILE), f32),
            pltpu.VMEM((ROWS, TILE), f32),
            pltpu.VMEM((16, TILE), f32),
            pltpu.VMEM((GY - 1, 16, TILE), f32),
            pltpu.VMEM((GX - 1, 16, TILE), f32),
            pltpu.VMEM((16, TILE), f32),
            pltpu.VMEM((TILE, 8, TILE), f32),
            pltpu.VMEM((1, TILE), f32),
            pltpu.VMEM((1, TILE), f32),
            pltpu.VMEM((GX * GY // 2 - 1, 1, TILE), f32),
            pltpu.VMEM((1, TILE), f32),
            pltpu.SemaphoreType.REGULAR((3,)),
            pltpu.SemaphoreType.DMA((6,)),
            pltpu.SemaphoreType.DMA((8,)),
            pltpu.SemaphoreType.DMA((8,)),
            pltpu.SemaphoreType.DMA((5,)),
            pltpu.SemaphoreType.DMA((5,)),
        ],
        compiler_params=pltpu.CompilerParams(
            collective_id=0, has_side_effects=True, vmem_limit_bytes=40 << 20
        ),
        name="flow_and_gram",
    )(*(pltpu.with_memory_space_constraint(x, pltpu.HBM) for x in (flow_state, sound_speed_sq, snapshots)))


def body(flow_state, sound_speed_sq, snapshots):
    new_state, block, early, normal, late = first(flow_state, sound_speed_sq, snapshots)
    local = pl.BlockSpec(memory_space=pltpu.VMEM)
    anywhere = pl.BlockSpec(memory_space=pl.ANY)
    hbm = pl.BlockSpec(memory_space=pltpu.HBM)
    f32 = jnp.float32
    pod_basis, new_state = pl.pallas_call(
        basis_kernel,
        out_shape=(
            jax.ShapeDtypeStruct((MODES, TILE, TILE), f32),
            jax.ShapeDtypeStruct((4, TILE, TILE), f32),
        ),
        in_specs=[local] * 4 + [anywhere],
        out_specs=(hbm, hbm),
        scratch_shapes=[
            pltpu.VMEM((MODES, TILE, TILE), f32),
            pltpu.SemaphoreType.DMA((TILE // 8,)),
            pltpu.SemaphoreType.DMA,
        ],
        compiler_params=pltpu.CompilerParams(vmem_limit_bytes=20 << 20),
        name="basis",
    )(early, normal, late, block, new_state)
    return new_state, pod_basis


def solution(mesh):
    placed = (P(None, "gx", "gy"), P("gx", "gy"), P(None, "gx", "gy"))
    return jax.shard_map(
        body,
        mesh=mesh,
        in_specs=placed,
        out_specs=(P(None, "gx", "gy"), P(None, "gx", "gy")),
        check_vma=False,
    )
```

```python
import jax
import jax.numpy as jnp
from jax import lax
from jax.experimental import pallas as pl
from jax.experimental.pallas import tpu as pltpu
from jax.sharding import PartitionSpec as P

MESH = pl.DeviceIdType.MESH
STEPS = 2
courant = 0.8
stream_speed = 0.3
span_speed = 0.1

MODES = 64
RESIDENT = 62
TILE = 128
EARLY_ROWS = 64
HALO = 12
PAD = 16
ROWS = TILE + 2 * PAD
FIELDS = 5
GX = 32
GY = 8


def lanes(shape):
    return lax.broadcasted_iota(jnp.int32, shape, len(shape) - 1)


def slope_rows(ref, window, field, row, rows):
    near = ref[window, field, pl.ds(row + 1, rows), :] - ref[window, field, pl.ds(row - 1, rows), :]
    far = ref[window, field, pl.ds(row + 2, rows), :] - ref[window, field, pl.ds(row - 2, rows), :]
    return 8.0 * near - far


def slope_lanes(value):
    near = pltpu.roll(value, TILE - 1, 1) - pltpu.roll(value, 1, 1)
    far = pltpu.roll(value, TILE - 2, 1) - pltpu.roll(value, 2, 1)
    return 8.0 * near - far


def lane_band():
    away = lax.rem(
        lax.broadcasted_iota(jnp.int32, (TILE, TILE), 0) - lanes((TILE, TILE)) + TILE, TILE
    )
    band = jnp.where(away == 1, 8.0, jnp.where(away == TILE - 1, -8.0, 0.0))
    band = jnp.where(away == 2, -1.0, jnp.where(away == TILE - 2, 1.0, band)).astype(jnp.bfloat16)
    return jnp.concatenate([band, band, band], axis=0)


def split(value):
    high = value.astype(jnp.bfloat16)
    rest = value - high.astype(jnp.float32)
    middle = rest.astype(jnp.bfloat16)
    return [high, middle, (rest - middle.astype(jnp.float32)).astype(jnp.bfloat16)]


def stage(kind, margin, state, source, target, sound, band):
    scale = courant / 12.0
    row, end = PAD - margin, PAD + TILE + margin
    while row < end:
        rows = 16 if end - row > 8 else 8
        here = pl.ds(row, rows)
        for w in range(2):
            centre = [source[w, f, here, :] for f in range(4)]
            dx = [slope_rows(source, w, f, row, rows) for f in range(4)]
            pair = jnp.concatenate(split(jnp.concatenate(centre[2:], axis=0)), axis=1)
            pair = jnp.dot(pair, band, preferred_element_type=jnp.float32)
            dy = [slope_lanes(centre[0]), slope_lanes(centre[1]), pair[:rows], pair[rows:]]
            diverge = dx[1] + dy[2]
            advect = [stream_speed * dx[f] + span_speed * dy[f] for f in range(4)]
            rate = [
                advect[0] + diverge,
                advect[1] + dx[3],
                advect[2] + dy[3],
                advect[3] + sound[w, 4, here, :] * diverge,
            ]
            for f in range(4):
                if kind == 1:
                    moved = centre[f] - scale * rate[f]
                elif kind == 2:
                    moved = 0.75 * state[w, f, here, :] + (0.25 * centre[f] - (0.25 * scale) * rate[f])
                else:
                    moved = (1.0 / 3.0) * state[w, f, here, :] + (
                        (2.0 / 3.0) * centre[f] - (2.0 / 3.0 * scale) * rate[f]
                    )
                target[w, f, here, :] = moved
        row += rows


def joined(wide, field, row, rows):
    here = pl.ds(PAD + row, rows)
    lane = lanes((rows, TILE))
    first = (lane >= HALO) & (lane < 64)
    both = jnp.where(first, wide[0, field, here, :], wide[1, field, here, :])
    return pltpu.roll(both, TILE - HALO, 1)


def spread(row):
    return jnp.broadcast_to(row, (8, TILE))


def inverse_factor(gram):
    count = MODES // 8
    lane, sub = lanes((8, TILE)), lax.broadcasted_iota(jnp.int32, (8, TILE), 0)
    tiles = [
        jnp.where(lane < MODES, gram[8 * r : 8 * r + 8], jnp.where(lane == MODES + 8 * r + sub, 1.0, 0.0))
        for r in range(count)
    ]
    for t in range(count):
        column = {
            (j, r): jnp.broadcast_to(tiles[r][:, 8 * t + j : 8 * t + j + 1], (8, TILE))
            for j in range(8)
            for r in range(t, count)
        }
        for j in range(0, 8, 2):
            corner, side = spread(column[j, t][j : j + 1, :]), spread(column[j + 1, t][j : j + 1, :])
            below, other = spread(column[j, t][j + 1 : j + 2, :]), spread(column[j + 1, t][j + 1 : j + 2, :])
            inverse_first = 1.0 / corner
            inverse_second = corner * (1.0 / (corner * other - below * side))
            ratio = below * inverse_first
            first = {r: column[j, r] * inverse_first for r in range(t, count)}
            first[t] = jnp.where(sub > j, first[t], 0.0)
            second = {r: (column[j + 1, r] - first[r] * side) * inverse_second for r in range(t, count)}
            second[t] = jnp.where(sub > j + 1, second[t], 0.0)
            for later in range(j + 2, 8):
                upper = spread(column[later, t][j : j + 1, :])
                lower = spread(column[later, t][j + 1 : j + 2, :]) - ratio * upper
                for r in range(t, count):
                    column[later, r] = column[later, r] - first[r] * upper - second[r] * lower
            upper = spread(tiles[t][j : j + 1, :])
            lower = spread(tiles[t][j + 1 : j + 2, :]) - ratio * upper
            for r in range(t, count):
                tiles[r] = tiles[r] - first[r] * upper - second[r] * lower
    rows = []
    for r in range(count):
        diagonal = jnp.sum(jnp.where(lane == 8 * r + sub, tiles[r], 0.0), axis=1, keepdims=True)
        scaled = pltpu.roll(tiles[r] * (1.0 / jnp.sqrt(diagonal)), MODES, 1)
        rows.append(jnp.where(lane < MODES, scaled, 0.0))
    return jnp.concatenate(rows, axis=0)


def fold(gram):
    half = MODES // 2
    wide = jnp.concatenate([gram, jnp.zeros_like(gram)], axis=1)
    early, late = wide[:half], wide[half:]
    row, lane = lax.broadcasted_iota(jnp.int32, (half, TILE), 0), lanes((half, TILE))
    diagonal = jnp.sum(jnp.where(lane == row + half, late, 0.0), axis=0, keepdims=True)
    mixed = jnp.where((lane >= half) & (lane <= row + half), pltpu.roll(early, half, 1), late)
    mixed = jnp.where((row == RESIDENT - half) & (lane < half), pltpu.roll(diagonal, TILE - half, 1), mixed)
    return mixed[: half // 2] + pltpu.roll(mixed[half // 2 :], MODES, 1)


def unfold(folded):
    half = MODES // 2
    row, lane = lax.broadcasted_iota(jnp.int32, (half, TILE), 0), lanes((half, TILE))
    mixed = jnp.concatenate([folded, pltpu.roll(folded, MODES, 1)], axis=0)
    diagonal = pltpu.roll(mixed[RESIDENT - half : RESIDENT - half + 1], half, 1)
    empty = (lane >= MODES) | ((lane < half) & (row >= RESIDENT - half))
    mixed = jnp.where(empty, 0.0, mixed)
    early = jnp.where(lane <= row, pltpu.roll(mixed, TILE - half, 1), 0.0)
    late = jnp.where((lane < half) | (lane > row + half), mixed, 0.0)
    whole = jnp.concatenate([early, late], axis=0)
    turned = jnp.concatenate([whole[:, :MODES].T, jnp.zeros((MODES, MODES), jnp.float32)], axis=1)
    row, lane = lax.broadcasted_iota(jnp.int32, (MODES, TILE), 0), lanes((MODES, TILE))
    middle = jnp.where(row < half, whole, jnp.where(row < RESIDENT, diagonal, 1.0))
    return jnp.where(row == lane, middle, whole + turned)


def exact_dot(a, b, contract):
    return lax.dot_general(
        a, b, (contract, ((), ())), precision=lax.Precision.HIGHEST, preferred_element_type=jnp.float32
    )


def turn(snap, block, group, first=0, last=TILE):
    modes = pl.ds(group * 16, 16)
    for row in range(first, last, 16):
        turned = jnp.swapaxes(snap[modes, row : row + 16, :], 0, 1)
        for i in range(16):
            block[modes, (row + i) * TILE : (row + i + 1) * TILE] = turned[i]


def wide_kernel(
    flow_hbm, sound_hbm, snap_hbm, state_out, block, inverse_out, normal_out, late_out,
    snap, tile, wide, one, two, strip, left_strip, right_strip,
    packed, part_one, part_two, total_two,
    line, late, late_one, late_two, late_total,
    reach_sem, load_sem, halo_send, halo_recv, sum_send, sum_recv,
):
    gx, gy = lax.axis_index("gx"), lax.axis_index("gy")
    core = lax.rem(gy, 2)
    cells = GX * GY * TILE * TILE

    def at(dx, dy):
        return (lax.rem(gx + (dx + GX), GX), lax.rem(gy + (dy + GY), GY))

    x, z, y = gx // 8, lax.rem(gx, 8), gy // 2
    row_steps = sorted(
        ((dx, dz) for dx in range(4) for dz in range(8) if dx or dz),
        key=lambda step: -min(step[0], 4 - step[0]) - min(step[1], 8 - step[1]),
    )
    row_peers = [(lax.rem(x + dx, 4) * 8 + lax.rem(z + dz, 8), gy) for dx, dz in row_steps]
    column_steps = sorted(
        ((dy, dc) for dy in range(4) for dc in range(2) if dy or dc), key=lambda step: -min(step[0], 4 - step[0])
    )
    column_peers = [(gx, lax.rem(y + dy, 4) * 2 + lax.rem(core + dc, 2)) for dy, dc in column_steps]
    chip_steps = sorted(
        ((dx, dy, dz) for dx in range(4) for dy in range(4) for dz in range(8) if dx or dy or dz),
        key=lambda step: -min(step[0], 4 - step[0]) - min(step[1], 4 - step[1]) - min(step[2], 8 - step[2]),
    )
    chip_peers = [
        (lax.rem(x + dx, 4) * 8 + lax.rem(z + dz, 8), lax.rem(y + dy, 4) * 2 + core) for dx, dy, dz in chip_steps
    ]
    partner = (gx, gy + 1 - 2 * core)
    corner_peers = [at(dx, dy) for dx in (-1, 1) for dy in (-1, 1)]
    near_peers = [
        peer
        for (dx, dz), peer in zip(row_steps, row_peers)
        if min(dx, 4 - dx) + min(dz, 8 - dz) <= 2
    ]
    entered = near_peers + column_peers + corner_peers

    barrier = pltpu.get_barrier_semaphore()
    for peer in entered:
        pl.semaphore_signal(barrier, inc=1, device_id=peer, device_id_type=MESH)

    inside = pl.ds(PAD, TILE)
    loads = [
        pltpu.make_async_copy(flow_hbm, tile.at[pl.ds(0, 4), inside, :], load_sem.at[0]),
        pltpu.make_async_copy(sound_hbm, tile.at[4, inside, :], load_sem.at[1]),
    ] + [
        pltpu.make_async_copy(
            snap_hbm.at[:, pl.ds(part * 32, 32), :],
            snap.at[pl.ds(0, RESIDENT), pl.ds(part * 32, 32), :],
            load_sem.at[2 + part],
        )
        for part in range(4)
    ]
    for load in loads:
        load.start()
    line[...] = jnp.zeros((TILE, 8, TILE), jnp.float32)
    snap[RESIDENT:MODES] = jnp.zeros((MODES - RESIDENT, TILE, TILE), jnp.bfloat16)
    loads[0].wait()
    loads[1].wait()

    lane = lanes((16, TILE))
    for row in range(0, TILE, 16):
        gathered = pltpu.roll(tile[0, pl.ds(PAD + row, 16), :], HALO, 1)
        for f in range(1, FIELDS):
            moved = pltpu.roll(tile[f, pl.ds(PAD + row, 16), :], HALO + 24 * f, 1)
            gathered = jnp.where(lane >= 24 * f, moved, gathered)
        strip[pl.ds(row, 16), :] = gathered

    def products(first, last, so_far):
        for row in range(first, last, 16):
            if row % 32 == 0:
                loads[2 + row // 32].wait()
            for group in range(4):
                turn(snap, block, group, row, row + 16)
            piece = block[:, row * TILE : (row + 16) * TILE]
            so_far = so_far + lax.dot_general(
                piece, piece, (((1,), (1,)), ((), ())), preferred_element_type=jnp.float32
            )
        return so_far

    gram = products(0, EARLY_ROWS, jnp.zeros((MODES, MODES), jnp.float32))
    pl.semaphore_wait(barrier, len(entered))

    top, bottom = pl.ds(0, PAD), pl.ds(PAD + TILE, PAD)
    low, high = pl.ds(0, PAD), pl.ds(TILE - PAD, PAD)
    moves = [
        (tile.at[:, pl.ds(TILE, PAD), :], tile.at[:, top, :], at(1, 0)),
        (tile.at[:, pl.ds(PAD, PAD), :], tile.at[:, bottom, :], at(-1, 0)),
        (strip, left_strip.at[inside, :], at(0, 1)),
        (strip, right_strip.at[inside, :], at(0, -1)),
        (strip.at[high, :], left_strip.at[top, :], at(1, 1)),
        (strip.at[low, :], left_strip.at[bottom, :], at(-1, 1)),
        (strip.at[high, :], right_strip.at[top, :], at(1, -1)),
        (strip.at[low, :], right_strip.at[bottom, :], at(-1, -1)),
    ]
    halos = []
    for number, (source, target, peer) in enumerate(moves):
        halos.append(
            pltpu.make_async_remote_copy(
                src_ref=source, dst_ref=target, send_sem=halo_send.at[number],
                recv_sem=halo_recv.at[number], device_id=peer, device_id_type=MESH,
            )
        )
        halos[-1].start()

    def send(source, target, slot, peer):
        copy = pltpu.make_async_remote_copy(
            src_ref=source, dst_ref=target, send_sem=sum_send.at[slot],
            recv_sem=sum_recv.at[slot], device_id=peer, device_id_type=MESH,
        )
        copy.start()
        return copy

    def received(ref, slot):
        pltpu.make_async_copy(ref, ref, sum_recv.at[slot]).wait()

    def sent(ref, slot):
        pltpu.make_async_copy(ref, ref, sum_send.at[slot]).wait()

    def pass_on(step, peers):
        for peer in peers:
            pl.semaphore_signal(reach_sem.at[step], inc=1, device_id=peer, device_id_type=MESH)

    pass_on(0, near_peers)

    gram = products(EARLY_ROWS, TILE, gram) * (1.0 / cells)
    packed[...] = fold(gram)

    for number, peer in enumerate(column_peers):
        send(packed, part_one.at[number], 0, peer)

    pl.semaphore_wait(reach_sem.at[0], len(near_peers))
    pass_on(1, near_peers)
    for row in range(PAD, PAD + TILE, 16):
        for f in range(FIELDS):
            wide[0, f, pl.ds(row, 16), :] = pltpu.roll(tile[f, pl.ds(row, 16), :], HALO, 1)
    for halo in halos:
        halo.wait()
    for row in range(0, ROWS, 16):
        here = pl.ds(row, 16)
        main = PAD <= row < PAD + TILE
        merged = jnp.where(lax.rem(lane, 24) >= HALO, right_strip[here, :], left_strip[here, :])
        for f in range(FIELDS):
            beside = pltpu.roll(merged, TILE - 24 * f, 1) if f else merged
            turned = wide[0, f, here, :] if main else pltpu.roll(tile[f, here, :], HALO, 1)
            wide[0, f, here, :] = jnp.where(lane < HALO, beside, turned)
            wide[1, f, here, :] = jnp.where((lane >= HALO) & (lane < 2 * HALO), beside, turned)

    band = lane_band()
    stage(1, 10, wide, wide, one, wide, band)

    received(part_one, 0)
    total = packed[...]
    for number in range(GY - 1):
        total = total + part_one[number]
    total_two[...] = total
    pl.semaphore_wait(reach_sem.at[1], len(near_peers))
    pass_on(2, column_peers)
    for number, peer in enumerate(row_peers):
        send(total_two, part_two.at[number], 1, peer)

    stage(2, 8, wide, one, two, wide, band)
    stage(3, 6, wide, two, wide, wide, band)
    pressures = [joined(wide, 3, 0, TILE).astype(jnp.bfloat16)]
    snap[RESIDENT] = pressures[0]
    pressures[0] = pressures[0].astype(jnp.float32)
    line[:, 0, :] = pressures[0]
    stage(1, 4, wide, wide, one, wide, band)
    stage(2, 2, wide, one, two, wide, band)
    stage(3, 0, wide, two, wide, wide, band)
    pressures.append(joined(wide, 3, 0, TILE).astype(jnp.bfloat16))
    snap[RESIDENT + 1] = pressures[1]
    pressures[1] = pressures[1].astype(jnp.float32)
    line[:, 1, :] = pressures[1]

    flat = jnp.concatenate([line[i].astype(jnp.bfloat16) for i in range(TILE)], axis=1)
    fresh = lax.dot_general(flat, block[...], (((1,), (1,)), ((), ())), preferred_element_type=jnp.float32)

    def product(a, b):
        return jnp.sum(jnp.sum(pressures[a] * pressures[b], axis=0, keepdims=True), axis=1, keepdims=True)

    pair = jnp.concatenate([fresh[0:1], fresh[1:2]], axis=1)
    place = lanes((1, TILE))
    for where, value in ((62, product(0, 0)), (126, product(0, 1)), (127, product(1, 1))):
        pair = jnp.where(place == where, value, pair)
    late[...] = pair * (1.0 / cells)
    swap = send(late, late_one, 3, partner)

    pl.semaphore_wait(reach_sem.at[2], len(column_peers))
    swap.wait()
    late_total[...] = late[...] + late_one[...]
    for number, peer in enumerate(chip_peers):
        send(late_total, late_two.at[number], 4, peer)

    turn(snap, block, 3)
    for f in range(4):
        state_out[f] = joined(wide, f, 0, TILE)

    received(part_two, 1)
    total = total_two[...]
    for number in range(GX - 1):
        total = total + part_two[number]

    early = inverse_factor(unfold(total))
    inverse_out[...] = early
    normal_out[...] = exact_dot(early, early, ((0,), (0,)))

    received(late_two, 4)
    parts = [late_two[number] for number in range(8)]
    for number in range(8, len(chip_peers)):
        parts[number % 8] = parts[number % 8] + late_two[number]
    while len(parts) > 1:
        parts = [a + b for a, b in zip(parts[::2], parts[1::2])]
    late_out[...] = late_total[...] + parts[0]

    sent(part_one, 0)
    sent(part_two, 1)
    sent(late_two, 4)


def last_rows(early, normal, pair):
    lane = lanes((1, TILE))
    first = jnp.where(lane < MODES, pair, 0.0)
    second = jnp.where(lane < MODES, pltpu.roll(pair, MODES, 1), 0.0)

    def pick(vector, place):
        return jnp.sum(jnp.where(lane == place, vector, 0.0), axis=1, keepdims=True)

    norm_first, norm_second, cross = pick(first, 62), pick(second, 63), pick(second, 62)
    known = lane < RESIDENT
    both = jnp.concatenate(
        [jnp.where(known, first, 0.0), jnp.where(known, second, 0.0), jnp.zeros((6, TILE), jnp.float32)], axis=0
    )
    along = exact_dot(both, early, ((1,), (1,)))
    back = exact_dot(both, normal, ((1,), (0,)))
    along_first, along_second = along[0:1], along[1:2]
    scale_first = 1.0 / jnp.sqrt(norm_first - jnp.sum(along_first * along_first, axis=1, keepdims=True))
    row_first = (jnp.where(lane == 62, 1.0, 0.0) - back[0:1]) * scale_first
    shared = (cross - jnp.sum(along_first * along_second, axis=1, keepdims=True)) * scale_first
    left = norm_second - jnp.sum(along_second * along_second, axis=1, keepdims=True) - shared * shared
    row_second = (jnp.where(lane == 63, 1.0, 0.0) - back[1:2] - shared * row_first) * (1.0 / jnp.sqrt(left))
    return row_first, row_second


def basis_kernel(
    early_ref, normal_ref, late_ref, block_ref, state_hbm, basis_hbm, state_out, basis, sem, state_sem
):
    def weights(rows):
        return jnp.concatenate(split(rows[:, :MODES]), axis=1)

    def slab(number, weight):
        part = block_ref[:, number * 8 * TILE : (number + 1) * 8 * TILE]
        rows = jnp.dot(weight, jnp.concatenate([part, part, part], axis=0), preferred_element_type=jnp.float32)
        stacked = jnp.stack([rows[:, i * TILE : (i + 1) * TILE] for i in range(8)], axis=0)
        here = pl.ds(number * 8, 8)
        basis[:, here, :] = jnp.swapaxes(stacked, 0, 1)
        copy = pltpu.make_async_copy(basis.at[:, here, :], basis_hbm.at[:, here, :], sem.at[number])
        copy.start()
        return copy

    early = early_ref[...]
    row_first, row_second = last_rows(early, normal_ref[...], late_ref[...])
    weight = weights(jnp.concatenate([early[:RESIDENT], row_first, row_second], axis=0))
    copies = [slab(number, weight) for number in range(TILE // 8)]
    copies.append(pltpu.make_async_copy(state_hbm, state_out, state_sem))
    copies[-1].start()
    for copy in copies:
        copy.wait()


def first(flow_state, sound_speed_sq, snapshots):
    hbm = pl.BlockSpec(memory_space=pltpu.HBM)
    local = pl.BlockSpec(memory_space=pltpu.VMEM)
    f32, bf16 = jnp.float32, jnp.bfloat16
    wide = pltpu.VMEM((2, 4, ROWS, TILE), f32)
    return pl.pallas_call(
        wide_kernel,
        out_shape=(
            jax.ShapeDtypeStruct((4, TILE, TILE), f32),
            jax.ShapeDtypeStruct((MODES, TILE * TILE), bf16),
            jax.ShapeDtypeStruct((MODES, TILE), f32),
            jax.ShapeDtypeStruct((TILE, TILE), f32),
            jax.ShapeDtypeStruct((1, TILE), f32),
        ),
        in_specs=[hbm] * 3,
        out_specs=(local,) * 5,
        scratch_shapes=[
            pltpu.VMEM((MODES, TILE, TILE), bf16),
            pltpu.VMEM((FIELDS, ROWS, TILE), f32),
            pltpu.VMEM((2, FIELDS, ROWS, TILE), f32),
            wide,
            wide,
            pltpu.VMEM((TILE, TILE), f32),
            pltpu.VMEM((ROWS, TILE), f32),
            pltpu.VMEM((ROWS, TILE), f32),
            pltpu.VMEM((16, TILE), f32),
            pltpu.VMEM((GY - 1, 16, TILE), f32),
            pltpu.VMEM((GX - 1, 16, TILE), f32),
            pltpu.VMEM((16, TILE), f32),
            pltpu.VMEM((TILE, 8, TILE), f32),
            pltpu.VMEM((1, TILE), f32),
            pltpu.VMEM((1, TILE), f32),
            pltpu.VMEM((GX * GY // 2 - 1, 1, TILE), f32),
            pltpu.VMEM((1, TILE), f32),
            pltpu.SemaphoreType.REGULAR((3,)),
            pltpu.SemaphoreType.DMA((6,)),
            pltpu.SemaphoreType.DMA((8,)),
            pltpu.SemaphoreType.DMA((8,)),
            pltpu.SemaphoreType.DMA((5,)),
            pltpu.SemaphoreType.DMA((5,)),
        ],
        compiler_params=pltpu.CompilerParams(
            collective_id=0, has_side_effects=True, vmem_limit_bytes=40 << 20
        ),
        name="flow_and_gram",
    )(*(pltpu.with_memory_space_constraint(x, pltpu.HBM) for x in (flow_state, sound_speed_sq, snapshots)))


def body(flow_state, sound_speed_sq, snapshots):
    new_state, block, early, normal, late = first(flow_state, sound_speed_sq, snapshots)
    local = pl.BlockSpec(memory_space=pltpu.VMEM)
    anywhere = pl.BlockSpec(memory_space=pl.ANY)
    hbm = pl.BlockSpec(memory_space=pltpu.HBM)
    f32 = jnp.float32
    pod_basis, new_state = pl.pallas_call(
        basis_kernel,
        out_shape=(
            jax.ShapeDtypeStruct((MODES, TILE, TILE), f32),
            jax.ShapeDtypeStruct((4, TILE, TILE), f32),
        ),
        in_specs=[local] * 4 + [anywhere],
        out_specs=(hbm, hbm),
        scratch_shapes=[
            pltpu.VMEM((MODES, TILE, TILE), f32),
            pltpu.SemaphoreType.DMA((TILE // 8,)),
            pltpu.SemaphoreType.DMA,
        ],
        compiler_params=pltpu.CompilerParams(vmem_limit_bytes=20 << 20),
        name="basis",
    )(early, normal, late, block, new_state)
    return new_state, pod_basis


def solution(mesh):
    placed = (P(None, "gx", "gy"), P("gx", "gy"), P(None, "gx", "gy"))
    return jax.shard_map(
        body,
        mesh=mesh,
        in_specs=placed,
        out_specs=(P(None, "gx", "gy"), P(None, "gx", "gy")),
        check_vma=False,
    )
```
